32 devices in a mesh: grp: 2 (over y), row: 4 (over z), col: 2 (over x), frm: 2 (over core).
Axes of the slice: x: 2, y: 2, z: 4, core: 2. Of those that a mesh axis runs over, the one named last changes fastest.
Arguments:
- latent: bfloat16 [4, 16, 320, 256], P(('grp', 'frm'), 'row', 'col'), parts along dimension 0, may hold values from -6 to 6
- proj_weight: bfloat16 [256, 128], replicated, may hold values from -0.375 to 0.375
- proj_bias: float32 [128], replicated, may hold values from -3 to 3
- cache_one: bfloat16 [4, 32, 640, 128], P(('grp', 'frm'), 'row', 'col'), parts along dimension 0, may hold values from -6 to 6
- cache_two: bfloat16 [4, 32, 640, 128], P(('grp', 'frm'), 'row', 'col'), parts along dimension 0, may hold values from -6 to 6
- conv_one: bfloat16 [3, 3, 3, 128, 128], replicated, may hold values from -0.109375 to 0.109375
- bias_one: float32 [128], replicated, may hold values from -3 to 3
- conv_two: bfloat16 [3, 3, 3, 128, 128], replicated, may hold values from -0.109375 to 0.109375
- bias_two: float32 [128], replicated, may hold values from -3 to 3
Outputs:
- decoded: bfloat16 [4, 32, 640, 128], P(('grp', 'frm'), 'row', 'col'), parts along dimension 0
The draws below stay inside these ranges and needn't reach their ends.
There are 2 independent parts, one for each index of `grp`. The reference program is written for one: setup_inputs(seed, part) draws one part's arguments, and reference() takes and returns one part's arrays. A program takes and returns all parts, laid end to end along the dimension named above; an argument that names none is the same for every part. Nothing has to cross between parts.
All inputs are finite; a program needn't handle non-finite values.
Results may differ from the reference program's by a relative error of at most 0.0044.
Values may be sent and summed in bfloat16 or wider, within the bound.
A program may use at most 64 MiB of HBM per device.

```python
import jax
import jax.numpy as jnp

LCH = 256
CH = 128
FRAMES = 2
H = 32
W = 640
LH = 16
LW = 320


def block_scale(rng, extent, shards, least, top_value):
    loudness = 1.0
    for dim, parts in shards:
        steps = jax.random.uniform(jax.random.fold_in(jax.random.fold_in(rng, 6), dim), (parts,), jnp.float32, least / len(shards), top_value / len(shards))
        loudness = loudness * jnp.repeat(jnp.exp(steps), extent[dim] // parts).reshape((-1,) + (1,) * (len(extent) - 1 - dim))
    return loudness


def centred(rng, dims, scale, limit, split=(), dtype=jnp.bfloat16):
    gain = block_scale(rng, dims, split, -0.22, 0.18) if split else 1.0
    values = jax.random.normal(rng, dims, jnp.float32) * scale * gain
    return jnp.minimum(jnp.maximum(values, -limit), limit).astype(dtype)


def setup_inputs(seed: int = 0, part: int = 0) -> dict:
    keys = jax.random.split(jax.random.key(seed), 10)
    own_keys = jax.random.split(jax.random.fold_in(keys[9], part), 10)
    latent = centred(own_keys[0], (FRAMES, LH, LW, LCH), 1.0, 6.0, ((0, 2), (1, 4), (2, 2)))
    proj_weight = centred(keys[1], (LCH, CH), LCH ** -0.5, 0.375)
    proj_bias = centred(keys[2], (CH,), 0.5, 3.0, (), jnp.float32)
    cache_one = centred(own_keys[3], (FRAMES, H, W, CH), 1.0, 6.0, ((0, 2), (1, 4), (2, 2)))
    cache_two = centred(own_keys[4], (FRAMES, H, W, CH), 1.0, 6.0, ((0, 2), (1, 4), (2, 2)))
    conv_one = centred(keys[5], (3, 3, 3, CH, CH), (27 * CH) ** -0.5, 0.109375)
    bias_one = centred(keys[6], (CH,), 0.5, 3.0, (), jnp.float32)
    conv_two = centred(keys[7], (3, 3, 3, CH, CH), (27 * CH) ** -0.5, 0.109375)
    bias_two = centred(keys[8], (CH,), 0.5, 3.0, (), jnp.float32)
    return {"latent": latent, "proj_weight": proj_weight, "proj_bias": proj_bias, "cache_one": cache_one, "cache_two": cache_two, "conv_one": conv_one, "bias_one": bias_one, "conv_two": conv_two, "bias_two": bias_two}


def causal_conv(frames, weight, bias):
    tile_rows, tile_cols, channels = frames.shape[1], frames.shape[2], frames.shape[3]
    padded = jnp.pad(frames, ((0, 0), (1, 1), (1, 1), (0, 0)))
    folded = weight.reshape(3, 3, 3 * channels, weight.shape[-1])
    results = []
    for frame_out in range(frames.shape[0] - 2):
        summed = jnp.zeros((tile_rows * tile_cols, weight.shape[-1]), jnp.float32)
        for frame_step in range(3):
            for row_step in range(3):
                stencil = jnp.concatenate(
                    [padded[frame_out + frame_step, row_step:row_step + tile_rows, col_step:col_step + tile_cols]
                     for col_step in range(3)], axis=-1).reshape(tile_rows * tile_cols, 3 * channels)
                summed = summed + jnp.dot(stencil, folded[frame_step, row_step], preferred_element_type=jnp.float32)
        results.append((summed + bias).reshape(tile_rows, tile_cols, -1))
    return jnp.stack(results)


def reference(latent, proj_weight, proj_bias, cache_one, cache_two, conv_one, bias_one, conv_two, bias_two):
    projected = jnp.dot(latent.reshape(-1, latent.shape[-1]), proj_weight, preferred_element_type=jnp.float32) + proj_bias
    projected = projected.reshape(latent.shape[0], latent.shape[1], latent.shape[2], -1)
    upsampled = jnp.repeat(jnp.repeat(projected.astype(jnp.bfloat16), 2, axis=1), 2, axis=2)
    act_one = jax.nn.silu(upsampled.astype(jnp.float32)).astype(jnp.bfloat16)
    first_out = causal_conv(jnp.concatenate([cache_one, act_one], axis=0), conv_one, bias_one)
    act_two = jax.nn.silu(first_out).astype(jnp.bfloat16)
    second_out = causal_conv(jnp.concatenate([cache_two, act_two], axis=0), conv_two, bias_two)
    return (upsampled.astype(jnp.float32) + second_out).astype(jnp.bfloat16)
```

```python
import functools

import jax
import jax.numpy as jnp
from jax import lax
from jax.experimental import pallas as pl
from jax.experimental.pallas import tpu as pltpu
from jax.sharding import PartitionSpec as P

EDGE = 16
MESH = pl.DeviceIdType.MESH
SIDES = [(-1, 0), (1, 0), (0, -1), (0, 1), (-1, -1), (-1, 1), (1, -1), (1, 1)]
ONE, COARSE, TWO = 0, 1, 2
MIDDLE = (1, 0, 1)


def kernel(rows_n, cols_n, lat_h, pw_h, pb_h, c1_h, c2_h, w1_h, b1_h, w2_h, b2_h, out_h,
           lat, pw, w, wu, F1, CA, CB, F2, up, obuf, acc1, acc2, s1, ps, pr, pb, b1, b2,
           load_sem, side_send, side_recv, cross_send, cross_recv,
           mid_send, mid_recv, part_send, part_recv, out_sem):
    R, W, CH = c1_h.shape[1], c1_h.shape[2], c1_h.shape[3]
    HR, HW = lat.shape[0], lat.shape[1]
    WP, HP = W + 2 * EDGE, HW + 2 * EDGE
    bf, f32 = jnp.bfloat16, jnp.float32
    r, c, f = lax.axis_index("row"), lax.axis_index("col"), lax.axis_index("frm")
    up_ok, down_ok = r > 0, r < rows_n - 1
    left_ok, right_ok = c > 0, c < cols_n - 1
    first, second = f == 0, f == 1

    def exists(d):
        dr, dc = SIDES[d]
        ok = None
        for test in ([up_ok] if dr < 0 else [down_ok] if dr > 0 else []) + (
                [left_ok] if dc < 0 else [right_ok] if dc > 0 else []):
            ok = test if ok is None else jnp.logical_and(ok, test)
        return ok

    def where_is(d):
        dr, dc = SIDES[d]
        ids = {}
        if dr:
            ids["row"] = r + dr
        if dc:
            ids["col"] = c + dc
        return ids

    def opposite(d):
        return SIDES.index((-SIDES[d][0], -SIDES[d][1]))

    loads = []

    def load(src, dst):
        cp = pltpu.make_async_copy(src, dst, load_sem.at[len(loads)])
        cp.start()
        loads.append(cp)
        return cp

    def load_weights(cv, src):
        return [load(src.at[:, :, q], w.at[cv, :, :, :, pl.ds(q * CH, CH)]) for q in range(3)]

    first_cp = [load(lat_h.at[0], lat), load(pw_h, pw), load(pb_h, pb)]
    w_cp = [load_weights(0, w1_h)]
    cache_cp = [load(c1_h.at[0], F1.at[0, pl.ds(1, R), pl.ds(0, W)])]
    w_cp.append(load_weights(1, w2_h))
    cache_cp.append(load(c2_h.at[0], F2.at[0, pl.ds(1, R), pl.ds(0, W)]))
    bias_cp = [load(b1_h, b1), load(b2_h, b2)]

    partner = {"frm": 1 - f}
    barrier = pltpu.get_barrier_semaphore()
    for d in range(8):
        @pl.when(exists(d))
        def _():
            pl.semaphore_signal(barrier, inc=1, device_id=where_is(d), device_id_type=MESH)
            if SIDES[d][0] == 0:
                pl.semaphore_signal(barrier, inc=1, device_id={**where_is(d), **partner},
                                    device_id_type=MESH)
    pl.semaphore_signal(barrier, inc=1, device_id=partner, device_id_type=MESH)

    def clear(ref, *place):
        shape = ref.at[place].shape
        ref[place] = jnp.zeros(shape, bf)

    rims = ((left_ok, lambda n: pl.ds(n - EDGE, EDGE)), (right_ok, lambda n: pl.ds(n - 2 * EDGE, EDGE)))
    for ref, tall, wide in ((F1.at[0], R, WP), (CA, HR, HP)):
        for ok, row in ((up_ok, 0), (down_ok, tall + 1)):
            @pl.when(jnp.logical_not(ok))
            def _():
                clear(ref, row, pl.ds(0, wide))
        for ok, rim in rims:
            @pl.when(jnp.logical_not(ok))
            def _():
                clear(ref, pl.ds(0, tall + 2), rim(wide))
    for ok, rim in rims:
        @pl.when(jnp.logical_not(ok))
        def _():
            clear(F2, 0, pl.ds(1, R), rim(WP))

            @pl.when(first)
            def _():
                clear(F1, 1, pl.ds(1, R), rim(WP))
                clear(F2, 1, pl.ds(1, R), rim(WP))

            @pl.when(second)
            def _():
                clear(CB, pl.ds(1, HR), rim(HP))
    for a in range(3):
        for row in (0, R + 1):
            clear(F2, a, row, pl.ds(0, WP))

    for cp in first_cp:
        cp.wait()

    def project(i, carry):
        v = jnp.dot(lat[i], pw[...], preferred_element_type=f32) + pb[...]
        v = v.astype(bf).astype(f32)
        CA[1 + i, pl.ds(0, HW)] = (v / (1.0 + jnp.exp(-v))).astype(bf)
        for k in range(2):
            s1[pl.ds(k, HW, stride=2), :] = v
        up[i] = s1[...].astype(bf)
        return carry

    lax.fori_loop(0, HR, project, 0)

    tall = 1 + up_ok.astype(jnp.int32) + down_ok.astype(jnp.int32)
    wide = 1 + left_ok.astype(jnp.int32) + right_ok.astype(jnp.int32)
    pl.semaphore_wait(barrier, tall * wide + wide - 1)

    def side_refs(cv, d, slot=0):
        dr, dc = SIDES[d]
        n, m = (HR, HW) if cv == COARSE else (R, W)
        row, land_row = (0, n + 1) if dr < 0 else (n - 1, 0)
        col, land_col = ((0, m) if dc < 0 else (m - EDGE, m + EDGE))
        rows, land_rows = (pl.ds(row, 1), pl.ds(land_row, 1)) if dr else (pl.ds(0, n), pl.ds(1, n))
        cols, land_cols = (
            (pl.ds(col, EDGE), pl.ds(land_col, EDGE)) if dc else (pl.ds(0, m), pl.ds(0, m)))
        if cv == COARSE:
            src = CA.at[pl.ds(1 + rows.start, rows.size), cols]
            return src, (CB if slot else CA).at[land_rows, land_cols]
        src = (c1_h, c2_h)[cv // 2].at[0, rows, cols]
        return src, (F1, F2)[cv // 2].at[slot, land_rows, land_cols]

    def side_copy(cv, d):
        src, dst = side_refs(cv, d)
        return pltpu.make_async_remote_copy(
            src_ref=src, dst_ref=dst, send_sem=side_send.at[cv, d], recv_sem=side_recv.at[cv, d],
            device_id=where_is(d), device_id_type=MESH)

    def cross_copy(cv, d):
        src, dst = side_refs(cv, d, 1)
        return pltpu.make_async_remote_copy(
            src_ref=src, dst_ref=dst, send_sem=cross_send.at[cv, d - 2],
            recv_sem=cross_recv.at[cv, d - 2], device_id={**where_is(d), **partner},
            device_id_type=MESH)

    tall_ds, col_ds = (0, 1, 4, 5, 6, 7), (2, 3)

    def sides(act, cv, ds):
        for d in ds:
            @pl.when(exists(opposite(d) if act == "recv" else d))
            def _():
                cp = side_copy(cv, d)
                {"start": cp.start, "recv": cp.wait_recv, "send": cp.wait_send}[act]()

    def cross(act, cv):
        owner = f == MIDDLE[cv]
        for d in col_ds:
            there = exists(opposite(d) if act == "recv" else d)

            @pl.when(jnp.logical_and(there, jnp.logical_not(owner) if act == "recv" else owner))
            def _():
                cp = cross_copy(cv, d)
                {"start": cp.start, "recv": cp.wait_recv, "send": cp.wait_send}[act]()

    def to_partner(cv, k, src, dst):
        return pltpu.make_async_remote_copy(
            src_ref=src, dst_ref=dst, send_sem=mid_send.at[cv, k], recv_sem=mid_recv.at[cv, k],
            device_id=partner, device_id_type=MESH)

    all_w, all_h = pl.ds(0, WP), pl.ds(0, HP)
    to_first = [
        to_partner(0, 0, c1_h.at[0], F1.at[1, pl.ds(1, R), pl.ds(0, W)]),
        to_partner(0, 1, F1.at[0, 0, all_w], F1.at[1, 0, all_w]),
        to_partner(0, 2, F1.at[0, R + 1, all_w], F1.at[1, R + 1, all_w]),
        to_partner(1, 0, c2_h.at[0], F2.at[1, pl.ds(1, R), pl.ds(0, W)])]
    main = pl.ds(1, HR), pl.ds(0, HW)
    to_second = [
        to_partner(0, 0, CA.at[main], CB.at[main]),
        to_partner(0, 1, CA.at[0, all_h], CB.at[0, all_h]),
        to_partner(0, 2, CA.at[HR + 1, all_h], CB.at[HR + 1, all_h]),
        to_partner(1, 0, F2.at[2, 1, all_w], F2.at[1, 1, all_w]),
        to_partner(1, 1, F2.at[2, R, all_w], F2.at[1, R, all_w]),
        to_partner(1, 2, F2.at[2, pl.ds(2, R - 2), all_w], F2.at[1, pl.ds(2, R - 2), all_w])]

    def when_first(*bodies):
        @pl.when(first)
        def _():
            for body in bodies:
                body()

    def when_second(*bodies):
        @pl.when(second)
        def _():
            for body in bodies:
                body()

    sides("start", ONE, col_ds)
    cross("start", ONE)
    sides("start", ONE, tall_ds)
    when_second(to_first[0].start)
    when_first(to_second[0].start)
    sides("start", COARSE, range(8))
    cross("start", COARSE)
    when_second(to_first[3].start)
    sides("start", TWO, col_ds)
    cross("start", TWO)

    def weights(cv, frames):
        return jnp.concatenate([w[cv, a].reshape(3 * CH, 3 * CH) for a in frames], axis=0)

    def fold_taps(place, a):
        k0, k1, k2 = (w[0, a, p].astype(f32) for p in range(3))
        for parity, pair in ((0, (k0, k1 + k2)), (1, (k0 + k1, k2))):
            for b, m in enumerate(pair):
                q0, q1, q2 = m[:, :CH], m[:, CH:2 * CH], m[:, 2 * CH:]
                wu[parity, pl.ds((2 * place + b) * CH, CH)] = jnp.concatenate(
                    [q1 + q2, q0 + q1, q0, q2], axis=1).astype(bf)

    for cp in w_cp[0]:
        cp.wait()
    fold_taps(0, 2)
    when_second(lambda: fold_taps(1, 1))

    spot = lax.broadcasted_iota(jnp.int32, (8, CH), 0)

    def fold_main(z):
        after = pltpu.roll(z[:, :CH], 1, 0)
        after = jnp.concatenate([jnp.where(spot == 0, 0.0, after[:8]), after[8:]], axis=0)
        ahead = pltpu.roll(z[:, 2 * CH:], W - 1, 0)
        ahead = jnp.concatenate([ahead[:W - 8], jnp.where(spot == 7, 0.0, ahead[W - 8:])], axis=0)
        return after + z[:, CH:2 * CH] + ahead

    def fold_ring(z):
        n = z.shape[0]
        return pltpu.roll(z[:, :CH], 1, 0) + z[:, CH:2 * CH] + pltpu.roll(z[:, 2 * CH:], n - 1, 0)

    def second_main(frames):
        lhs = jnp.concatenate(
            [F2[a, pl.ds(p, R), pl.ds(0, W)].reshape(R * W, CH) for a in frames for p in range(3)],
            axis=1)
        z = jnp.dot(lhs, weights(1, frames), preferred_element_type=f32)
        return [fold_main(z[n * W:(n + 1) * W]) for n in range(R)]

    cache_cp[1].wait()
    for cp in w_cp[1]:
        cp.wait()
    for n, y in enumerate(second_main((0,))):
        acc2[n] = y

    def first_rows(frames, spans):
        lhs = jnp.concatenate(
            [jnp.concatenate([F1[a, pl.ds(at + p, n)].reshape(n * WP, CH)
                              for a in frames for p in range(3)], axis=1) for at, n in spans],
            axis=0)
        z = jnp.dot(lhs, weights(0, frames), preferred_element_type=f32)
        rows = [at + k for at, n in spans for k in range(n)]
        for k, row in enumerate(rows):
            acc1[pl.ds(row * WP, WP)] = fold_ring(z[k * WP:(k + 1) * WP])

    inside, border = [(1, R - 2)], [(0, 1), (R - 1, 1)]
    cache_cp[0].wait()
    for cp in bias_cp:
        cp.wait()
    sides("recv", ONE, col_ds)
    cross("recv", ONE)
    when_first(to_first[0].wait_recv, lambda: first_rows((0, 1), inside))
    when_second(lambda: first_rows((0,), inside))

    sides("recv", ONE, tall_ds)
    when_second(to_first[1].start, to_first[2].start)
    sides("recv", COARSE, range(8))
    when_first(to_second[1].start, to_second[2].start)
    cross("recv", COARSE)
    when_first(to_first[1].wait_recv, to_first[2].wait_recv, lambda: first_rows((0, 1), border))
    when_second(lambda: first_rows((0,), border))

    def coarse(frames):
        for parity in range(2):
            lhs = jnp.concatenate(
                [ref[pl.ds(parity + b, HR)].reshape(HR * HP, CH) for ref in frames for b in range(2)],
                axis=1)
            z = jnp.dot(lhs, wu[parity, pl.ds(0, 2 * CH * len(frames))], preferred_element_type=f32)
            for i in range(HR):
                zi = z[i * HP:(i + 1) * HP]
                even = zi[:, :CH] + pltpu.roll(zi[:, 2 * CH:3 * CH], 1, 0)
                odd = zi[:, CH:2 * CH] + pltpu.roll(zi[:, 3 * CH:], HP - 1, 0)
                base = (2 * i + parity) * WP
                for at, n, to in ((0, HW, 0), (HW, EDGE // 2, W), (HP - EDGE // 2, EDGE // 2, WP - EDGE)):
                    for k, y in ((0, even), (1, odd)):
                        acc1[pl.ds(base + to + k, n, stride=2), :] += y[at:at + n]

    when_first(lambda: coarse((CA,)))
    when_second(lambda: [cp.wait_recv() for cp in to_second[:3]], lambda: coarse((CA, CB)))

    def act_two(row):
        y = acc1[pl.ds(row * WP, WP)] + b1[...]
        y = y / (1.0 + jnp.exp(-y))
        F2[2, 1 + row, pl.ds(0, W)] = y[:W].astype(bf)
        F2[2, 1 + row, pl.ds(W, EDGE)] = jnp.where(right_ok, y[W:W + EDGE], 0.0).astype(bf)
        F2[2, 1 + row, pl.ds(W + EDGE, EDGE)] = jnp.where(left_ok, y[W + EDGE:], 0.0).astype(bf)

    for k in range(2):
        act_two(k * (R - 1))
    when_first(to_second[3].start, to_second[4].start)

    def inner(k, carry):
        act_two(1 + k)
        return carry

    lax.fori_loop(0, R - 2, inner, 0)
    when_first(to_second[5].start)

    sides("recv", TWO, col_ds)
    cross("recv", TWO)
    when_first(to_first[3].wait_recv)
    when_second(to_second[3].wait_recv, to_second[4].wait_recv)

    def part_copy(k):
        return pltpu.make_async_remote_copy(
            src_ref=ps.at[k], dst_ref=pr.at[1 - k], send_sem=part_send.at[k],
            recv_sem=part_recv.at[1 - k], device_id={"row": r - 1 + 2 * k}, device_id_type=MESH)

    reach = (up_ok, down_ok)
    for k in range(2):
        @pl.when(reach[k])
        def _():
            lhs = jnp.concatenate([F2[a, 1 + k * (R - 1)] for a in range(3)], axis=1)
            rhs = jnp.concatenate([w[1, a, 2 - 2 * k] for a in range(3)], axis=0)
            z = fold_ring(jnp.dot(lhs, rhs, preferred_element_type=f32))
            ps[k] = z[:W].astype(bf)
            part_copy(k).start()

    when_second(to_second[5].wait_recv)
    for n, y in enumerate(second_main((1, 2))):
        acc2[n] += y

    lhs = jnp.concatenate(
        [F2[a, pl.ds(p, R), pl.ds(W, 2 * EDGE)].reshape(R * 2 * EDGE, CH)
         for a in range(3) for p in range(3)], axis=1)
    z = jnp.dot(lhs, weights(1, range(3)), preferred_element_type=f32)
    for n in range(R):
        part = z[n * 2 * EDGE:(n + 1) * 2 * EDGE]
        acc2[n, pl.ds(0, 1)] += part[2 * EDGE - 1:, :CH]
        acc2[n, pl.ds(W - 1, 1)] += part[:1, 2 * CH:]

    def out_copy(i):
        return pltpu.make_async_copy(obuf.at[i], out_h.at[0, i], out_sem.at[i])

    def finish(row):
        y = acc2[row] + b2[...] + up[row // 2].astype(f32)
        obuf[row] = y.astype(bf)
        out_copy(row).start()

    def last(k, carry):
        finish(1 + k)
        return carry

    lax.fori_loop(0, R - 2, last, 0)
    for k in range(2):
        row = k * (R - 1)

        @pl.when(reach[k])
        def _():
            part_copy(1 - k).wait_recv()
            acc2[row] += pr[k].astype(f32)

        finish(row)

    for cv, ds in ((ONE, range(8)), (COARSE, range(8)), (TWO, col_ds)):
        sides("send", cv, ds)
        cross("send", cv)
    when_second(*[cp.wait_send for cp in to_first])
    when_first(*[cp.wait_send for cp in to_second])
    for k in range(2):
        @pl.when(reach[k])
        def _():
            part_copy(k).wait_send()
    for i in range(R):
        out_copy(i).wait()


def per_device(latent, proj_weight, proj_bias, cache_one, cache_two,
               conv_one, bias_one, conv_two, bias_two):
    _, R, W, CH = cache_one.shape
    _, HR, HW, LCH = latent.shape
    WP, HP = W + 2 * EDGE, HW + 2 * EDGE
    anywhere = pl.BlockSpec(memory_space=pl.ANY)
    bf, f32 = jnp.bfloat16, jnp.float32
    dma = pltpu.SemaphoreType.DMA
    return pl.pallas_call(
        functools.partial(kernel, lax.axis_size("row"), lax.axis_size("col")),
        out_shape=jax.ShapeDtypeStruct(cache_one.shape, bf),
        in_specs=[anywhere] * 9,
        out_specs=anywhere,
        scratch_shapes=[
            pltpu.VMEM((HR, HW, LCH), bf),
            pltpu.VMEM((LCH, CH), bf),
            pltpu.VMEM((2, 3, 3, CH, 3 * CH), bf),
            pltpu.VMEM((2, 4 * CH, 4 * CH), bf),
            pltpu.VMEM((2, R + 2, WP, CH), bf),
            pltpu.VMEM((HR + 2, HP, CH), bf),
            pltpu.VMEM((HR + 2, HP, CH), bf),
            pltpu.VMEM((3, R + 2, WP, CH), bf),
            pltpu.VMEM((HR, W, CH), bf),
            pltpu.VMEM((R, W, CH), bf),
            pltpu.VMEM((R * WP, CH), f32),
            pltpu.VMEM((R, W, CH), f32),
            pltpu.VMEM((W, CH), f32),
            pltpu.VMEM((2, W, CH), bf),
            pltpu.VMEM((2, W, CH), bf),
            pltpu.VMEM((1, CH), f32),
            pltpu.VMEM((1, CH), f32),
            pltpu.VMEM((1, CH), f32),
            dma((13,)), dma((3, 8)), dma((3, 8)), dma((3, 2)), dma((3, 2)),
            dma((2, 3)), dma((2, 3)), dma((2,)), dma((2,)), dma((R,)),
        ],
        compiler_params=pltpu.CompilerParams(
            collective_id=0, has_side_effects=True, vmem_limit_bytes=56 * 1024 * 1024),
        name="decoder_window",
    )(latent, proj_weight, proj_bias.reshape(1, CH), cache_one, cache_two,
      conv_one, bias_one.reshape(1, CH), conv_two, bias_two.reshape(1, CH))


def solution(mesh):
    placed = P(("grp", "frm"), "row", "col", None)
    return jax.shard_map(
        per_device,
        mesh=mesh,
        in_specs=(placed, P(), P(), placed, placed, P(), P(), P(), P()),
        out_specs=placed,
        check_vma=False,
    )
```

```python
import functools

import jax
import jax.numpy as jnp
from jax import lax
from jax.experimental import pallas as pl
from jax.experimental.pallas import tpu as pltpu
from jax.sharding import PartitionSpec as P

EDGE = 16
MESH = pl.DeviceIdType.MESH
ONE, COARSE, TWO = 0, 1, 2
MIDDLE = (1, 0, 1)


def kernel(rows_n, cols_n, lat_h, pw_h, pb_h, c1_h, c2_h, w1_h, b1_h, w2_h, b2_h, out_v,
           lat, pw, w, wu, F1, CA, CB, F2, up, acc1, acc2, part, s1, ps1, pr1, ps2, pr2, pb, b1, b2,
           load_sem, side_send, side_recv, mid_send, mid_recv, part_send, part_recv):
    R, W, CH = c1_h.shape[1], c1_h.shape[2], c1_h.shape[3]
    HR, HW = lat.shape[0], lat.shape[1]
    WP, HP = W + 2 * EDGE, HW + 2 * EDGE
    bf, f32 = jnp.bfloat16, jnp.float32
    r, c, f = lax.axis_index("row"), lax.axis_index("col"), lax.axis_index("frm")
    up_ok, down_ok = r > 0, r < rows_n - 1
    left_ok, right_ok = c > 0, c < cols_n - 1
    first, second = f == 0, f == 1

    beside, reach = (left_ok, right_ok), (up_ok, down_ok)

    loads = []

    def load(src, dst):
        cp = pltpu.make_async_copy(src, dst, load_sem.at[len(loads)])
        cp.start()
        loads.append(cp)
        return cp

    def load_weights(cv, src):
        return [load(src.at[:, :, q], w.at[cv, :, :, :, pl.ds(q * CH, CH)]) for q in range(3)]

    first_cp = [load(lat_h.at[0], lat), load(pw_h, pw), load(pb_h, pb)]
    two_cp = [load(c2_h.at[0], F2.at[0, pl.ds(1, R), pl.ds(0, W)])] + load_weights(1, w2_h)
    w_cp = load_weights(0, w1_h)
    one_cp = [load(c1_h.at[0], F1.at[0, pl.ds(1, R), pl.ds(0, W)]), load(b1_h, b1), load(b2_h, b2)]

    partner = {"frm": 1 - f}
    barrier = pltpu.get_barrier_semaphore()
    for k in range(2):
        @pl.when(reach[k])
        def _():
            pl.semaphore_signal(barrier, inc=1, device_id={"row": r - 1 + 2 * k}, device_id_type=MESH)

        @pl.when(beside[k])
        def _():
            for ids in ({}, partner):
                pl.semaphore_signal(barrier, inc=1, device_id={"col": c - 1 + 2 * k, **ids},
                                    device_id_type=MESH)
    pl.semaphore_signal(barrier, inc=1, device_id=partner, device_id_type=MESH)

    def clear(ref, *place):
        shape = ref.at[place].shape
        ref[place] = jnp.zeros(shape, bf)

    rims = ((left_ok, lambda n: pl.ds(n - EDGE, EDGE)), (right_ok, lambda n: pl.ds(n - 2 * EDGE, EDGE)))
    for ok, rim in rims:
        @pl.when(jnp.logical_not(ok))
        def _():
            for ref, n, wide in ((F1.at[0], R, WP), (F2.at[0], R, WP), (CA, HR, HP)):
                clear(ref, pl.ds(1, n), rim(wide))

            @pl.when(first)
            def _():
                clear(F1, 1, pl.ds(1, R), rim(WP))
                clear(F2, 1, pl.ds(1, R), rim(WP))

            @pl.when(second)
            def _():
                clear(CB, pl.ds(1, HR), rim(HP))
    for ref, n, wide in ([(F1.at[a], R, WP) for a in range(2)] + [(F2.at[a], R, WP) for a in range(3)]
                         + [(CA, HR, HP), (CB, HR, HP)]):
        for row in (0, n + 1):
            clear(ref, row, pl.ds(0, wide))

    for cp in first_cp:
        cp.wait()

    def project(i, carry):
        v = jnp.dot(lat[i], pw[...], preferred_element_type=f32) + pb[...]
        v = v.astype(bf).astype(f32)
        CA[1 + i, pl.ds(0, HW)] = (v / (1.0 + jnp.exp(-v))).astype(bf)
        for k in range(2):
            s1[pl.ds(k, HW, stride=2), :] = v
        up[i] = s1[...].astype(bf)
        return carry

    lax.fori_loop(0, HR, project, 0)

    def side_copy(cv, k, slot):
        n, m = (HR, HW) if cv == COARSE else (R, W)
        cols, land = pl.ds(k * (m - EDGE), EDGE), (pl.ds(1, n), pl.ds(m + k * EDGE, EDGE))
        if cv == COARSE:
            src, dst = CA.at[pl.ds(1, n), cols], (CB if slot else CA).at[land]
        else:
            src, dst = (c1_h, c2_h)[cv // 2].at[0, :, cols], (F1, F2)[cv // 2].at[(slot, *land)]
        return pltpu.make_async_remote_copy(
            src_ref=src, dst_ref=dst, send_sem=side_send.at[cv, slot, k],
            recv_sem=side_recv.at[cv, slot, k],
            device_id={"col": c - 1 + 2 * k, **(partner if slot else {})}, device_id_type=MESH)

    def sides(act, cv):
        owner = f == MIDDLE[cv]
        for k in range(2):
            there = beside[1 - k if act == "recv" else k]
            for slot in range(2):
                also = jnp.logical_not(owner) if act == "recv" else owner

                @pl.when(jnp.logical_and(there, also) if slot else there)
                def _():
                    cp = side_copy(cv, k, slot)
                    {"start": cp.start, "recv": cp.wait_recv, "send": cp.wait_send}[act]()

    def to_partner(cv, k, src, dst):
        return pltpu.make_async_remote_copy(
            src_ref=src, dst_ref=dst, send_sem=mid_send.at[cv, k], recv_sem=mid_recv.at[cv, k],
            device_id=partner, device_id_type=MESH)

    all_w = pl.ds(0, WP)
    to_first = [
        to_partner(0, 0, c1_h.at[0], F1.at[1, pl.ds(1, R), pl.ds(0, W)]),
        to_partner(1, 0, c2_h.at[0], F2.at[1, pl.ds(1, R), pl.ds(0, W)])]
    main = pl.ds(1, HR), pl.ds(0, HW)
    to_second = [
        to_partner(0, 0, CA.at[main], CB.at[main]),
        to_partner(1, 0, F2.at[2, 1, all_w], F2.at[1, 1, all_w]),
        to_partner(1, 1, F2.at[2, R, all_w], F2.at[1, R, all_w]),
        to_partner(1, 2, F2.at[2, pl.ds(2, R - 2), all_w], F2.at[1, pl.ds(2, R - 2), all_w])]

    def when_first(*bodies):
        @pl.when(first)
        def _():
            for body in bodies:
                body()

    def when_second(*bodies):
        @pl.when(second)
        def _():
            for body in bodies:
                body()

    def weights(cv, frames):
        return jnp.concatenate([w[cv, a].reshape(3 * CH, 3 * CH) for a in frames], axis=0)

    def fold_taps(place, a):
        k0, k1, k2 = (w[0, a, p].astype(f32) for p in range(3))
        for parity, pair in ((0, (k0, k1 + k2)), (1, (k0 + k1, k2))):
            for b, m in enumerate(pair):
                q0, q1, q2 = m[:, :CH], m[:, CH:2 * CH], m[:, 2 * CH:]
                wu[parity, pl.ds((2 * place + b) * CH, CH)] = jnp.concatenate(
                    [q1 + q2, q0 + q1, q0, q2], axis=1).astype(bf)

    spot = lax.broadcasted_iota(jnp.int32, (8, CH), 0)

    def fold_main(z):
        after = pltpu.roll(z[:, :CH], 1, 0)
        after = jnp.concatenate([jnp.where(spot == 0, 0.0, after[:8]), after[8:]], axis=0)
        ahead = pltpu.roll(z[:, 2 * CH:], W - 1, 0)
        ahead = jnp.concatenate([ahead[:W - 8], jnp.where(spot == 7, 0.0, ahead[W - 8:])], axis=0)
        return after + z[:, CH:2 * CH] + ahead

    def fold_ring(z):
        n = z.shape[0]
        return pltpu.roll(z[:, :CH], 1, 0) + z[:, CH:2 * CH] + pltpu.roll(z[:, 2 * CH:], n - 1, 0)

    def second_main(frames, at=0, size=R):
        lhs = jnp.concatenate(
            [F2[a, pl.ds(at + p, size), pl.ds(0, W)].reshape(size * W, CH)
             for a in frames for p in range(3)], axis=1)
        z = jnp.dot(lhs, weights(1, frames), preferred_element_type=f32)
        return [fold_main(z[n * W:(n + 1) * W]) for n in range(size)]

    def own_two(at, size):
        for n, y in enumerate(second_main((0,), at, size)):
            acc2[at + n] = y

    for cp in two_cp:
        cp.wait()
    own_two(0, R // 2)
    count = [ok.astype(jnp.int32) for ok in reach + beside + beside]
    pl.semaphore_wait(barrier, sum(count, 1))
    sides("start", ONE)
    sides("start", COARSE)
    when_second(to_first[0].start)
    when_first(to_second[0].start)
    sides("start", TWO)
    when_second(to_first[1].start)
    own_two(R // 2, R // 2)
    for cp in w_cp:
        cp.wait()
    fold_taps(0, 2)
    when_second(lambda: fold_taps(1, 1))

    def cached_one(frames):
        lhs = jnp.concatenate(
            [F1[a, pl.ds(p, R)].reshape(R * WP, CH) for a in frames for p in range(3)], axis=1)
        z = jnp.dot(lhs, weights(0, frames), preferred_element_type=f32)
        for n in range(R):
            acc1[pl.ds(n * WP, WP)] = fold_ring(z[n * WP:(n + 1) * WP])

    def spread(ref, base, z):
        even = z[:, :CH] + pltpu.roll(z[:, 2 * CH:3 * CH], 1, 0)
        odd = z[:, CH:2 * CH] + pltpu.roll(z[:, 3 * CH:], HP - 1, 0)
        half = EDGE // 2
        for at, n, to in ((0, HW, 0), (HW, half, W), (HP - half, half, WP - EDGE)):
            for k, y in ((0, even), (1, odd)):
                ref[pl.ds(base + to + k, n, stride=2), :] += y[at:at + n]

    def coarse(refs):
        for parity in range(2):
            lhs = jnp.concatenate(
                [ref[pl.ds(parity + b, HR)].reshape(HR * HP, CH) for ref in refs for b in range(2)],
                axis=1)
            z = jnp.dot(lhs, wu[parity, pl.ds(0, 2 * CH * len(refs))], preferred_element_type=f32)
            for i in range(HR):
                spread(acc1, (2 * i + parity) * WP, z[i * HP:(i + 1) * HP])

    def border_one(frames, refs):
        for k in range(2):
            row, low = k * WP, 1 - k
            lhs = jnp.concatenate([F1[a, 1 + k * (R - 1)] for a in frames], axis=1)
            rhs = jnp.concatenate([w[0, a, 2 * low] for a in frames], axis=0)
            part[pl.ds(row, WP)] = fold_ring(jnp.dot(lhs, rhs, preferred_element_type=f32))
            lhs = jnp.concatenate([ref[1 + k * (HR - 1)] for ref in refs], axis=1)
            rhs = jnp.concatenate(
                [wu[low, pl.ds((2 * i + low) * CH, CH)] for i in range(len(refs))], axis=0)
            spread(part, row, jnp.dot(lhs, rhs, preferred_element_type=f32))
            ps1[k] = part[pl.ds(row, WP)].astype(bf)

    def part_copy(cv, k):
        mine, theirs = ((ps1, pr1), (ps2, pr2))[cv]
        return pltpu.make_async_remote_copy(
            src_ref=mine.at[k], dst_ref=theirs.at[1 - k], send_sem=part_send.at[cv, k],
            recv_sem=part_recv.at[cv, 1 - k], device_id={"row": r - 1 + 2 * k}, device_id_type=MESH)

    def send_parts(cv):
        for k in range(2):
            @pl.when(reach[k])
            def _():
                part_copy(cv, k).start()

    for cp in one_cp:
        cp.wait()
    sides("recv", ONE)
    sides("recv", COARSE)
    when_first(to_first[0].wait_recv, lambda: border_one((0, 1), (CA,)))
    when_second(to_second[0].wait_recv, lambda: border_one((0,), (CA, CB)))
    send_parts(0)
    when_first(lambda: cached_one((0, 1)), lambda: coarse((CA,)))
    when_second(lambda: cached_one((0,)), lambda: coarse((CA, CB)))

    def act_two(row):
        y = acc1[pl.ds(row * WP, WP)] + b1[...]
        y = y / (1.0 + jnp.exp(-y))
        F2[2, 1 + row, pl.ds(0, W)] = y[:W].astype(bf)
        F2[2, 1 + row, pl.ds(W, EDGE)] = jnp.where(right_ok, y[W:W + EDGE], 0.0).astype(bf)
        F2[2, 1 + row, pl.ds(W + EDGE, EDGE)] = jnp.where(left_ok, y[W + EDGE:], 0.0).astype(bf)

    for k in range(2):
        @pl.when(reach[k])
        def _():
            part_copy(0, 1 - k).wait_recv()
            acc1[pl.ds(k * (R - 1) * WP, WP)] += pr1[k].astype(f32)

        act_two(k * (R - 1))
    when_first(to_second[1].start, to_second[2].start)

    def inner(k, carry):
        act_two(1 + k)
        return carry

    lax.fori_loop(0, R - 2, inner, 0)
    when_first(to_second[3].start)

    sides("recv", TWO)
    when_first(to_first[1].wait_recv)
    when_second(to_second[1].wait_recv, to_second[2].wait_recv)
    for k in range(2):
        lhs = jnp.concatenate([F2[a, 1 + k * (R - 1)] for a in range(3)], axis=1)
        rhs = jnp.concatenate([w[1, a, 2 - 2 * k] for a in range(3)], axis=0)
        ps2[k] = fold_ring(jnp.dot(lhs, rhs, preferred_element_type=f32))[:W].astype(bf)
    send_parts(1)

    when_second(to_second[3].wait_recv)
    for n, y in enumerate(second_main((1, 2))):
        acc2[n] += y

    lhs = jnp.concatenate(
        [F2[a, pl.ds(p, R), pl.ds(W, 2 * EDGE)].reshape(R * 2 * EDGE, CH)
         for a in range(3) for p in range(3)], axis=1)
    z = jnp.dot(lhs, weights(1, range(3)), preferred_element_type=f32)
    for n in range(R):
        part = z[n * 2 * EDGE:(n + 1) * 2 * EDGE]
        acc2[n, pl.ds(0, 1)] += part[2 * EDGE - 1:, :CH]
        acc2[n, pl.ds(W - 1, 1)] += part[:1, 2 * CH:]

    def finish(row):
        y = acc2[row] + b2[...] + up[row // 2].astype(f32)
        out_v[0, row] = y.astype(bf)

    def last(k, carry):
        finish(1 + k)
        return carry

    lax.fori_loop(0, R - 2, last, 0)
    for k in range(2):
        row = k * (R - 1)

        @pl.when(reach[k])
        def _():
            part_copy(1, 1 - k).wait_recv()
            acc2[row] += pr2[k].astype(f32)

        finish(row)

    for cv in (ONE, COARSE, TWO):
        sides("send", cv)
    when_second(*[cp.wait_send for cp in to_first])
    when_first(*[cp.wait_send for cp in to_second])
    for cv in range(2):
        for k in range(2):
            @pl.when(reach[k])
            def _():
                part_copy(cv, k).wait_send()


def store(src, dst, sem):
    cp = pltpu.make_async_copy(src, dst, sem)
    cp.start()
    cp.wait()


def per_device(latent, proj_weight, proj_bias, cache_one, cache_two,
               conv_one, bias_one, conv_two, bias_two):
    _, R, W, CH = cache_one.shape
    _, HR, HW, LCH = latent.shape
    WP, HP = W + 2 * EDGE, HW + 2 * EDGE
    anywhere = pl.BlockSpec(memory_space=pl.ANY)
    bf, f32 = jnp.bfloat16, jnp.float32
    dma = pltpu.SemaphoreType.DMA
    decoded = pl.pallas_call(
        functools.partial(kernel, lax.axis_size("row"), lax.axis_size("col")),
        out_shape=pltpu.VMEM(cache_one.shape, bf),
        in_specs=[anywhere] * 9,
        out_specs=pl.BlockSpec(memory_space=pltpu.VMEM),
        scratch_shapes=[
            pltpu.VMEM((HR, HW, LCH), bf),
            pltpu.VMEM((LCH, CH), bf),
            pltpu.VMEM((2, 3, 3, CH, 3 * CH), bf),
            pltpu.VMEM((2, 4 * CH, 4 * CH), bf),
            pltpu.VMEM((2, R + 2, WP, CH), bf),
            pltpu.VMEM((HR + 2, HP, CH), bf),
            pltpu.VMEM((HR + 2, HP, CH), bf),
            pltpu.VMEM((3, R + 2, WP, CH), bf),
            pltpu.VMEM((HR, W, CH), bf),
            pltpu.VMEM((R * WP, CH), f32),
            pltpu.VMEM((R, W, CH), f32),
            pltpu.VMEM((2 * WP, CH), f32),
            pltpu.VMEM((W, CH), f32),
            pltpu.VMEM((2, WP, CH), bf),
            pltpu.VMEM((2, WP, CH), bf),
            pltpu.VMEM((2, W, CH), bf),
            pltpu.VMEM((2, W, CH), bf),
            pltpu.VMEM((1, CH), f32),
            pltpu.VMEM((1, CH), f32),
            pltpu.VMEM((1, CH), f32),
            dma((13,)), dma((3, 2, 2)), dma((3, 2, 2)), dma((2, 3)), dma((2, 3)),
            dma((2, 2)), dma((2, 2)),
        ],
        compiler_params=pltpu.CompilerParams(
            collective_id=0, has_side_effects=True, vmem_limit_bytes=60 * 1024 * 1024),
        name="decoder_window",
    )(latent, proj_weight, proj_bias.reshape(1, CH), cache_one, cache_two,
      conv_one, bias_one.reshape(1, CH), conv_two, bias_two.reshape(1, CH))
    return pl.pallas_call(
        store,
        out_shape=jax.ShapeDtypeStruct(cache_one.shape, bf),
        in_specs=[pl.BlockSpec(memory_space=pltpu.VMEM)],
        out_specs=anywhere,
        scratch_shapes=[dma],
        compiler_params=pltpu.CompilerParams(vmem_limit_bytes=1024 * 1024),
        name="store",
    )(decoded)


def solution(mesh):
    placed = P(("grp", "frm"), "row", "col", None)
    return jax.shard_map(
        per_device,
        mesh=mesh,
        in_specs=(placed, P(), P(), placed, placed, P(), P(), P(), P()),
        out_specs=placed,
        check_vma=False,
    )
```

```python
import functools

import jax
import jax.numpy as jnp
from jax import lax
from jax.experimental import pallas as pl
from jax.experimental.pallas import tpu as pltpu
from jax.sharding import PartitionSpec as P

EDGE = 16
MESH = pl.DeviceIdType.MESH
SIDES = [(-1, 0), (1, 0), (0, -1), (0, 1), (-1, -1), (-1, 1), (1, -1), (1, 1)]
ONE, COARSE, TWO = 0, 1, 2
MIDDLE = (1, 0, 1)


def kernel(rows_n, cols_n, lat_h, pw_h, pb_h, c1_h, c2_h, w1_h, b1_h, w2_h, b2_h, out_v,
           lat, pw, w, wu, F1, CA, CB, F2, up, acc1, acc2, s1, ps, pr, pb, b1, b2,
           load_sem, side_send, side_recv, cross_send, cross_recv,
           mid_send, mid_recv, part_send, part_recv):
    R, W, CH = c1_h.shape[1], c1_h.shape[2], c1_h.shape[3]
    HR, HW = lat.shape[0], lat.shape[1]
    WP, HP = W + 2 * EDGE, HW + 2 * EDGE
    bf, f32 = jnp.bfloat16, jnp.float32
    r, c, f = lax.axis_index("row"), lax.axis_index("col"), lax.axis_index("frm")
    up_ok, down_ok = r > 0, r < rows_n - 1
    left_ok, right_ok = c > 0, c < cols_n - 1
    first, second = f == 0, f == 1

    def exists(d):
        dr, dc = SIDES[d]
        ok = None
        for test in ([up_ok] if dr < 0 else [down_ok] if dr > 0 else []) + (
                [left_ok] if dc < 0 else [right_ok] if dc > 0 else []):
            ok = test if ok is None else jnp.logical_and(ok, test)
        return ok

    def where_is(d):
        dr, dc = SIDES[d]
        ids = {}
        if dr:
            ids["row"] = r + dr
        if dc:
            ids["col"] = c + dc
        return ids

    def opposite(d):
        return SIDES.index((-SIDES[d][0], -SIDES[d][1]))

    loads = []

    def load(src, dst):
        cp = pltpu.make_async_copy(src, dst, load_sem.at[len(loads)])
        cp.start()
        loads.append(cp)
        return cp

    def load_weights(cv, src):
        return [load(src.at[:, :, q], w.at[cv, :, :, :, pl.ds(q * CH, CH)]) for q in range(3)]

    first_cp = [load(lat_h.at[0], lat), load(pw_h, pw), load(pb_h, pb)]
    two_cp = [load(c2_h.at[0], F2.at[0, pl.ds(1, R), pl.ds(0, W)])] + load_weights(1, w2_h)
    w_cp = load_weights(0, w1_h)
    one_cp = [load(c1_h.at[0], F1.at[0, pl.ds(1, R), pl.ds(0, W)]), load(b1_h, b1), load(b2_h, b2)]

    partner = {"frm": 1 - f}
    barrier = pltpu.get_barrier_semaphore()
    for d in range(8):
        @pl.when(exists(d))
        def _():
            for ids in ({}, partner):
                pl.semaphore_signal(barrier, inc=1, device_id={**where_is(d), **ids},
                                    device_id_type=MESH)
    pl.semaphore_signal(barrier, inc=1, device_id=partner, device_id_type=MESH)

    def clear(ref, *place):
        shape = ref.at[place].shape
        ref[place] = jnp.zeros(shape, bf)

    rims = ((left_ok, lambda n: pl.ds(n - EDGE, EDGE)), (right_ok, lambda n: pl.ds(n - 2 * EDGE, EDGE)))
    def clear_outside(ref, tall, wide):
        for ok, row in ((up_ok, 0), (down_ok, tall + 1)):
            @pl.when(jnp.logical_not(ok))
            def _():
                clear(ref, row, pl.ds(0, wide))
        for ok, rim in rims:
            @pl.when(jnp.logical_not(ok))
            def _():
                clear(ref, pl.ds(0, tall + 2), rim(wide))

    clear_outside(F1.at[0], R, WP)
    clear_outside(CA, HR, HP)

    @pl.when(second)
    def _():
        clear_outside(CB, HR, HP)

    for ok, rim in rims:
        @pl.when(jnp.logical_not(ok))
        def _():
            clear(F2, 0, pl.ds(1, R), rim(WP))

            @pl.when(first)
            def _():
                clear(F1, 1, pl.ds(1, R), rim(WP))
                clear(F2, 1, pl.ds(1, R), rim(WP))
    for a in range(3):
        for row in (0, R + 1):
            clear(F2, a, row, pl.ds(0, WP))

    for cp in first_cp:
        cp.wait()

    def project(i, carry):
        v = jnp.dot(lat[i], pw[...], preferred_element_type=f32) + pb[...]
        v = v.astype(bf).astype(f32)
        CA[1 + i, pl.ds(0, HW)] = (v / (1.0 + jnp.exp(-v))).astype(bf)
        for k in range(2):
            s1[pl.ds(k, HW, stride=2), :] = v
        up[i] = s1[...].astype(bf)
        return carry

    lax.fori_loop(0, HR, project, 0)

    def side_refs(cv, d, slot=0):
        dr, dc = SIDES[d]
        n, m = (HR, HW) if cv == COARSE else (R, W)
        row, land_row = (0, n + 1) if dr < 0 else (n - 1, 0)
        col, land_col = ((0, m) if dc < 0 else (m - EDGE, m + EDGE))
        rows, land_rows = (pl.ds(row, 1), pl.ds(land_row, 1)) if dr else (pl.ds(0, n), pl.ds(1, n))
        cols, land_cols = (
            (pl.ds(col, EDGE), pl.ds(land_col, EDGE)) if dc else (pl.ds(0, m), pl.ds(0, m)))
        if cv == COARSE:
            src = CA.at[pl.ds(1 + rows.start, rows.size), cols]
            return src, (CB if slot else CA).at[land_rows, land_cols]
        src = (c1_h, c2_h)[cv // 2].at[0, rows, cols]
        return src, (F1, F2)[cv // 2].at[slot, land_rows, land_cols]

    def side_copy(cv, d):
        src, dst = side_refs(cv, d)
        return pltpu.make_async_remote_copy(
            src_ref=src, dst_ref=dst, send_sem=side_send.at[cv, d], recv_sem=side_recv.at[cv, d],
            device_id=where_is(d), device_id_type=MESH)

    def cross_copy(cv, d):
        src, dst = side_refs(cv, d, 1)
        return pltpu.make_async_remote_copy(
            src_ref=src, dst_ref=dst, send_sem=cross_send.at[cv, d],
            recv_sem=cross_recv.at[cv, d], device_id={**where_is(d), **partner},
            device_id_type=MESH)

    tall_ds, col_ds = (0, 1, 4, 5, 6, 7), (2, 3)

    def sides(act, cv, ds):
        for d in ds:
            @pl.when(exists(opposite(d) if act == "recv" else d))
            def _():
                cp = side_copy(cv, d)
                {"start": cp.start, "recv": cp.wait_recv, "send": cp.wait_send}[act]()

    def cross(act, cv, ds):
        owner = f == MIDDLE[cv]
        for d in ds:
            there = exists(opposite(d) if act == "recv" else d)

            @pl.when(jnp.logical_and(there, jnp.logical_not(owner) if act == "recv" else owner))
            def _():
                cp = cross_copy(cv, d)
                {"start": cp.start, "recv": cp.wait_recv, "send": cp.wait_send}[act]()

    def to_partner(cv, k, src, dst):
        return pltpu.make_async_remote_copy(
            src_ref=src, dst_ref=dst, send_sem=mid_send.at[cv, k], recv_sem=mid_recv.at[cv, k],
            device_id=partner, device_id_type=MESH)

    all_w = pl.ds(0, WP)
    to_first = [
        to_partner(0, 0, c1_h.at[0], F1.at[1, pl.ds(1, R), pl.ds(0, W)]),
        to_partner(0, 1, F1.at[0, 0, all_w], F1.at[1, 0, all_w]),
        to_partner(0, 2, F1.at[0, R + 1, all_w], F1.at[1, R + 1, all_w]),
        to_partner(1, 0, c2_h.at[0], F2.at[1, pl.ds(1, R), pl.ds(0, W)])]
    main = pl.ds(1, HR), pl.ds(0, HW)
    to_second = [
        to_partner(0, 0, CA.at[main], CB.at[main]),
        to_partner(1, 0, F2.at[2, 1, all_w], F2.at[1, 1, all_w]),
        to_partner(1, 1, F2.at[2, R, all_w], F2.at[1, R, all_w]),
        to_partner(1, 2, F2.at[2, pl.ds(2, R - 2), all_w], F2.at[1, pl.ds(2, R - 2), all_w])]

    def when_first(*bodies):
        @pl.when(first)
        def _():
            for body in bodies:
                body()

    def when_second(*bodies):
        @pl.when(second)
        def _():
            for body in bodies:
                body()

    def weights(cv, frames):
        return jnp.concatenate([w[cv, a].reshape(3 * CH, 3 * CH) for a in frames], axis=0)

    def fold_taps(place, a):
        k0, k1, k2 = (w[0, a, p].astype(f32) for p in range(3))
        for parity, pair in ((0, (k0, k1 + k2)), (1, (k0 + k1, k2))):
            for b, m in enumerate(pair):
                q0, q1, q2 = m[:, :CH], m[:, CH:2 * CH], m[:, 2 * CH:]
                wu[parity, pl.ds((2 * place + b) * CH, CH)] = jnp.concatenate(
                    [q1 + q2, q0 + q1, q0, q2], axis=1).astype(bf)

    spot = lax.broadcasted_iota(jnp.int32, (8, CH), 0)

    def fold_main(z):
        after = pltpu.roll(z[:, :CH], 1, 0)
        after = jnp.concatenate([jnp.where(spot == 0, 0.0, after[:8]), after[8:]], axis=0)
        ahead = pltpu.roll(z[:, 2 * CH:], W - 1, 0)
        ahead = jnp.concatenate([ahead[:W - 8], jnp.where(spot == 7, 0.0, ahead[W - 8:])], axis=0)
        return after + z[:, CH:2 * CH] + ahead

    def fold_ring(z):
        n = z.shape[0]
        return pltpu.roll(z[:, :CH], 1, 0) + z[:, CH:2 * CH] + pltpu.roll(z[:, 2 * CH:], n - 1, 0)

    def second_main(frames, at=0, size=R):
        lhs = jnp.concatenate(
            [F2[a, pl.ds(at + p, size), pl.ds(0, W)].reshape(size * W, CH)
             for a in frames for p in range(3)], axis=1)
        z = jnp.dot(lhs, weights(1, frames), preferred_element_type=f32)
        return [fold_main(z[n * W:(n + 1) * W]) for n in range(size)]

    def own_two(at, size):
        for n, y in enumerate(second_main((0,), at, size)):
            acc2[at + n] = y

    tall = 1 + up_ok.astype(jnp.int32) + down_ok.astype(jnp.int32)
    wide = 1 + left_ok.astype(jnp.int32) + right_ok.astype(jnp.int32)
    pl.semaphore_wait(barrier, 2 * tall * wide - 1)
    when_second(lambda: sides("start", ONE, tall_ds))
    sides("start", ONE, col_ds)
    cross("start", ONE, col_ds)
    when_second(to_first[0].start)
    when_first(to_second[0].start)
    sides("start", COARSE, range(8))
    cross("start", COARSE, range(8))

    for cp in two_cp:
        cp.wait()
    own_two(0, R)
    when_first(lambda: sides("start", ONE, tall_ds))
    when_second(to_first[3].start)
    sides("start", TWO, col_ds)
    cross("start", TWO, col_ds)

    for cp in w_cp:
        cp.wait()
    fold_taps(0, 2)
    when_second(lambda: fold_taps(1, 1))

    def first_rows(frames, spans, add=False):
        lhs = jnp.concatenate(
            [jnp.concatenate([F1[a, pl.ds(at + p, n)].reshape(n * WP, CH)
                              for a in frames for p in range(3)], axis=1) for at, n in spans],
            axis=0)
        z = jnp.dot(lhs, weights(0, frames), preferred_element_type=f32)
        rows = [at + k for at, n in spans for k in range(n)]
        for k, row in enumerate(rows):
            y = fold_ring(z[k * WP:(k + 1) * WP])
            if add:
                acc1[pl.ds(row * WP, WP)] += y
            else:
                acc1[pl.ds(row * WP, WP)] = y

    def coarse(frames):
        for parity in range(2):
            lhs = jnp.concatenate(
                [ref[pl.ds(parity + b, HR)].reshape(HR * HP, CH) for ref in frames for b in range(2)],
                axis=1)
            z = jnp.dot(lhs, wu[parity, pl.ds(0, 2 * CH * len(frames))], preferred_element_type=f32)
            for i in range(HR):
                zi = z[i * HP:(i + 1) * HP]
                even = zi[:, :CH] + pltpu.roll(zi[:, 2 * CH:3 * CH], 1, 0)
                odd = zi[:, CH:2 * CH] + pltpu.roll(zi[:, 3 * CH:], HP - 1, 0)
                base = (2 * i + parity) * WP
                for at, n, to in ((0, HW, 0), (HW, EDGE // 2, W), (HP - EDGE // 2, EDGE // 2, WP - EDGE)):
                    for k, y in ((0, even), (1, odd)):
                        acc1[pl.ds(base + to + k, n, stride=2), :] += y[at:at + n]

    def act_two(row):
        y = acc1[pl.ds(row * WP, WP)] + b1[...]
        y = y / (1.0 + jnp.exp(-y))
        F2[2, 1 + row, pl.ds(0, W)] = y[:W].astype(bf)
        F2[2, 1 + row, pl.ds(W, EDGE)] = jnp.where(right_ok, y[W:W + EDGE], 0.0).astype(bf)
        F2[2, 1 + row, pl.ds(W + EDGE, EDGE)] = jnp.where(left_ok, y[W + EDGE:], 0.0).astype(bf)

    def inner(k, carry):
        act_two(1 + k)
        return carry

    def act_inside():
        lax.fori_loop(0, R - 2, inner, 0)

    inside, border = [(1, R - 2)], [(0, 1), (R - 1, 1)]
    for cp in one_cp:
        cp.wait()

    @pl.when(second)
    def _():
        sides("recv", ONE, tall_ds)
        to_first[1].start()
        to_first[2].start()
        sides("recv", ONE, col_ds)
        first_rows((0,), inside)
        first_rows((0,), border)
        sides("recv", COARSE, range(8))
        cross("recv", COARSE, range(8))
        to_second[0].wait_recv()
        coarse((CA, CB))

    @pl.when(first)
    def _():
        sides("recv", ONE, col_ds)
        cross("recv", ONE, col_ds)
        to_first[0].wait_recv()
        first_rows((0, 1), inside)
        for k in range(2):
            acc1[pl.ds(k * (R - 1) * WP, WP)] = jnp.zeros((WP, CH), f32)
        sides("recv", COARSE, range(8))
        coarse((CA,))
        act_inside()
        to_second[3].start()
        sides("recv", ONE, tall_ds)
        to_first[1].wait_recv()
        to_first[2].wait_recv()
        first_rows((0, 1), border, True)

    for k in range(2):
        act_two(k * (R - 1))
    when_first(to_second[1].start, to_second[2].start)

    when_second(act_inside)

    sides("recv", TWO, col_ds)
    cross("recv", TWO, col_ds)
    when_first(to_first[3].wait_recv)
    when_second(to_second[1].wait_recv, to_second[2].wait_recv)

    def part_copy(k):
        return pltpu.make_async_remote_copy(
            src_ref=ps.at[k], dst_ref=pr.at[1 - k], send_sem=part_send.at[k],
            recv_sem=part_recv.at[1 - k], device_id={"row": r - 1 + 2 * k}, device_id_type=MESH)

    reach = (up_ok, down_ok)
    for k in range(2):
        lhs = jnp.concatenate([F2[a, 1 + k * (R - 1)] for a in range(3)], axis=1)
        rhs = jnp.concatenate([w[1, a, 2 - 2 * k] for a in range(3)], axis=0)
        ps[k] = fold_ring(jnp.dot(lhs, rhs, preferred_element_type=f32))[:W].astype(bf)
    for k in range(2):
        @pl.when(reach[k])
        def _():
            part_copy(k).start()

    when_second(to_second[3].wait_recv)
    for n, y in enumerate(second_main((1, 2))):
        acc2[n] += y

    lhs = jnp.concatenate(
        [F2[a, pl.ds(p, R), pl.ds(W, 2 * EDGE)].reshape(R * 2 * EDGE, CH)
         for a in range(3) for p in range(3)], axis=1)
    z = jnp.dot(lhs, weights(1, range(3)), preferred_element_type=f32)
    for n in range(R):
        part = z[n * 2 * EDGE:(n + 1) * 2 * EDGE]
        acc2[n, pl.ds(0, 1)] += part[2 * EDGE - 1:, :CH]
        acc2[n, pl.ds(W - 1, 1)] += part[:1, 2 * CH:]

    def finish(row):
        y = acc2[row] + b2[...] + up[row // 2].astype(f32)
        out_v[0, row] = y.astype(bf)

    def last(k, carry):
        finish(1 + k)
        return carry

    lax.fori_loop(0, R - 2, last, 0)
    for k in range(2):
        row = k * (R - 1)

        @pl.when(reach[k])
        def _():
            part_copy(1 - k).wait_recv()
            acc2[row] += pr[k].astype(f32)

        finish(row)

    for cv, ds in ((ONE, range(8)), (COARSE, range(8)), (TWO, col_ds)):
        sides("send", cv, ds)
        cross("send", cv, range(8) if cv == COARSE else col_ds)
    when_second(*[cp.wait_send for cp in to_first])
    when_first(*[cp.wait_send for cp in to_second])
    for k in range(2):
        @pl.when(reach[k])
        def _():
            part_copy(k).wait_send()


def store(src, dst, sem):
    cp = pltpu.make_async_copy(src, dst, sem)
    cp.start()
    cp.wait()


def per_device(latent, proj_weight, proj_bias, cache_one, cache_two,
               conv_one, bias_one, conv_two, bias_two):
    _, R, W, CH = cache_one.shape
    _, HR, HW, LCH = latent.shape
    WP, HP = W + 2 * EDGE, HW + 2 * EDGE
    anywhere = pl.BlockSpec(memory_space=pl.ANY)
    bf, f32 = jnp.bfloat16, jnp.float32
    dma = pltpu.SemaphoreType.DMA
    decoded = pl.pallas_call(
        functools.partial(kernel, lax.axis_size("row"), lax.axis_size("col")),
        out_shape=pltpu.VMEM(cache_one.shape, bf),
        in_specs=[anywhere] * 9,
        out_specs=pl.BlockSpec(memory_space=pltpu.VMEM),
        scratch_shapes=[
            pltpu.VMEM((HR, HW, LCH), bf),
            pltpu.VMEM((LCH, CH), bf),
            pltpu.VMEM((2, 3, 3, CH, 3 * CH), bf),
            pltpu.VMEM((2, 4 * CH, 4 * CH), bf),
            pltpu.VMEM((2, R + 2, WP, CH), bf),
            pltpu.VMEM((HR + 2, HP, CH), bf),
            pltpu.VMEM((HR + 2, HP, CH), bf),
            pltpu.VMEM((3, R + 2, WP, CH), bf),
            pltpu.VMEM((HR, W, CH), bf),
            pltpu.VMEM((R * WP, CH), f32),
            pltpu.VMEM((R, W, CH), f32),
            pltpu.VMEM((W, CH), f32),
            pltpu.VMEM((2, W, CH), bf),
            pltpu.VMEM((2, W, CH), bf),
            pltpu.VMEM((1, CH), f32),
            pltpu.VMEM((1, CH), f32),
            pltpu.VMEM((1, CH), f32),
            dma((13,)), dma((3, 8)), dma((3, 8)), dma((3, 8)), dma((3, 8)),
            dma((2, 3)), dma((2, 3)), dma((2,)), dma((2,)),
        ],
        compiler_params=pltpu.CompilerParams(
            collective_id=0, has_side_effects=True, vmem_limit_bytes=60 * 1024 * 1024),
        name="decoder_window",
    )(latent, proj_weight, proj_bias.reshape(1, CH), cache_one, cache_two,
      conv_one, bias_one.reshape(1, CH), conv_two, bias_two.reshape(1, CH))
    return pl.pallas_call(
        store,
        out_shape=jax.ShapeDtypeStruct(cache_one.shape, bf),
        in_specs=[pl.BlockSpec(memory_space=pltpu.VMEM)],
        out_specs=anywhere,
        scratch_shapes=[dma],
        compiler_params=pltpu.CompilerParams(vmem_limit_bytes=1024 * 1024),
        name="store",
    )(decoded)


def solution(mesh):
    placed = P(("grp", "frm"), "row", "col", None)
    return jax.shard_map(
        per_device,
        mesh=mesh,
        in_specs=(placed, P(), P(), placed, placed, P(), P(), P(), P()),
        out_specs=placed,
        check_vma=False,
    )
```

```python
import functools

import jax
import jax.numpy as jnp
from jax import lax
from jax.experimental import pallas as pl
from jax.experimental.pallas import tpu as pltpu
from jax.sharding import PartitionSpec as P

EDGE = 16
MESH = pl.DeviceIdType.MESH
SIDES = [(-1, 0), (1, 0), (0, -1), (0, 1), (-1, -1), (-1, 1), (1, -1), (1, 1)]
ONE, COARSE, TWO = 0, 1, 2
MIDDLE = (1, 0, 1)


def kernel(rows_n, cols_n, lat_h, pw_h, pb_h, c1_h, c2_h, w1_h, b1_h, w2_h, b2_h, out_v,
           lat, pw, w, wu, F1, CA, CB, F2, up, acc1, acc2, s1, ps, pr, pb, b1, b2,
           load_sem, side_send, side_recv, cross_send, cross_recv,
           mid_send, mid_recv, part_send, part_recv):
    R, W, CH = c1_h.shape[1], c1_h.shape[2], c1_h.shape[3]
    HR, HW = lat.shape[0], lat.shape[1]
    WP, HP = W + 2 * EDGE, HW + 2 * EDGE
    bf, f32 = jnp.bfloat16, jnp.float32
    r, c, f = lax.axis_index("row"), lax.axis_index("col"), lax.axis_index("frm")
    up_ok, down_ok = r > 0, r < rows_n - 1
    left_ok, right_ok = c > 0, c < cols_n - 1
    first, second = f == 0, f == 1

    def exists(d):
        dr, dc = SIDES[d]
        ok = None
        for test in ([up_ok] if dr < 0 else [down_ok] if dr > 0 else []) + (
                [left_ok] if dc < 0 else [right_ok] if dc > 0 else []):
            ok = test if ok is None else jnp.logical_and(ok, test)
        return ok

    def where_is(d):
        dr, dc = SIDES[d]
        ids = {}
        if dr:
            ids["row"] = r + dr
        if dc:
            ids["col"] = c + dc
        return ids

    def opposite(d):
        return SIDES.index((-SIDES[d][0], -SIDES[d][1]))

    loads = []

    def load(src, dst):
        cp = pltpu.make_async_copy(src, dst, load_sem.at[len(loads)])
        cp.start()
        loads.append(cp)
        return cp

    def load_weights(cv, src):
        return [load(src.at[:, :, q], w.at[cv, :, :, :, pl.ds(q * CH, CH)]) for q in range(3)]

    first_cp = [load(lat_h.at[0], lat), load(pw_h, pw), load(pb_h, pb)]
    two_cp = [load(c2_h.at[0], F2.at[0, pl.ds(1, R), pl.ds(0, W)])] + load_weights(1, w2_h)
    w_cp = load_weights(0, w1_h)
    one_cp = [load(c1_h.at[0], F1.at[0, pl.ds(1, R), pl.ds(0, W)]), load(b1_h, b1), load(b2_h, b2)]

    partner = {"frm": 1 - f}
    barrier = pltpu.get_barrier_semaphore()
    for d in range(8):
        @pl.when(exists(d))
        def _():
            for ids in ({}, partner)[:2 if SIDES[d][0] == 0 else 1]:
                pl.semaphore_signal(barrier, inc=1, device_id={**where_is(d), **ids},
                                    device_id_type=MESH)
    pl.semaphore_signal(barrier, inc=1, device_id=partner, device_id_type=MESH)

    def clear(ref, *place):
        shape = ref.at[place].shape
        ref[place] = jnp.zeros(shape, bf)

    rims = ((left_ok, lambda n: pl.ds(n - EDGE, EDGE)), (right_ok, lambda n: pl.ds(n - 2 * EDGE, EDGE)))
    for ref, tall, wide in ((F1.at[0], R, WP), (CA, HR, HP)):
        for ok, row in ((up_ok, 0), (down_ok, tall + 1)):
            @pl.when(jnp.logical_not(ok))
            def _():
                clear(ref, row, pl.ds(0, wide))
        for ok, rim in rims:
            @pl.when(jnp.logical_not(ok))
            def _():
                clear(ref, pl.ds(0, tall + 2), rim(wide))
    for ok, rim in rims:
        @pl.when(jnp.logical_not(ok))
        def _():
            clear(F2, 0, pl.ds(1, R), rim(WP))

            @pl.when(first)
            def _():
                clear(F1, 1, pl.ds(1, R), rim(WP))
                clear(F2, 1, pl.ds(1, R), rim(WP))

            @pl.when(second)
            def _():
                clear(CB, pl.ds(1, HR), rim(HP))
    for a in range(3):
        for row in (0, R + 1):
            clear(F2, a, row, pl.ds(0, WP))

    for cp in first_cp:
        cp.wait()

    def project(i, carry):
        v = jnp.dot(lat[i], pw[...], preferred_element_type=f32) + pb[...]
        v = v.astype(bf).astype(f32)
        CA[1 + i, pl.ds(0, HW)] = (v / (1.0 + jnp.exp(-v))).astype(bf)
        for k in range(2):
            s1[pl.ds(k, HW, stride=2), :] = v
        up[i] = s1[...].astype(bf)
        return carry

    lax.fori_loop(0, HR, project, 0)

    def side_refs(cv, d, slot=0):
        dr, dc = SIDES[d]
        n, m = (HR, HW) if cv == COARSE else (R, W)
        row, land_row = (0, n + 1) if dr < 0 else (n - 1, 0)
        col, land_col = ((0, m) if dc < 0 else (m - EDGE, m + EDGE))
        rows, land_rows = (pl.ds(row, 1), pl.ds(land_row, 1)) if dr else (pl.ds(0, n), pl.ds(1, n))
        cols, land_cols = (
            (pl.ds(col, EDGE), pl.ds(land_col, EDGE)) if dc else (pl.ds(0, m), pl.ds(0, m)))
        if cv == COARSE:
            src = CA.at[pl.ds(1 + rows.start, rows.size), cols]
            return src, (CB if slot else CA).at[land_rows, land_cols]
        src = (c1_h, c2_h)[cv // 2].at[0, rows, cols]
        return src, (F1, F2)[cv // 2].at[slot, land_rows, land_cols]

    def side_copy(cv, d):
        src, dst = side_refs(cv, d)
        return pltpu.make_async_remote_copy(
            src_ref=src, dst_ref=dst, send_sem=side_send.at[cv, d], recv_sem=side_recv.at[cv, d],
            device_id=where_is(d), device_id_type=MESH)

    def cross_copy(cv, d):
        src, dst = side_refs(cv, d, 1)
        return pltpu.make_async_remote_copy(
            src_ref=src, dst_ref=dst, send_sem=cross_send.at[cv, d - 2],
            recv_sem=cross_recv.at[cv, d - 2], device_id={**where_is(d), **partner},
            device_id_type=MESH)

    tall_ds, col_ds = (0, 1, 4, 5, 6, 7), (2, 3)

    def sides(act, cv, ds):
        for d in ds:
            @pl.when(exists(opposite(d) if act == "recv" else d))
            def _():
                cp = side_copy(cv, d)
                {"start": cp.start, "recv": cp.wait_recv, "send": cp.wait_send}[act]()

    def cross(act, cv, ds):
        owner = f == MIDDLE[cv]
        for d in ds:
            there = exists(opposite(d) if act == "recv" else d)

            @pl.when(jnp.logical_and(there, jnp.logical_not(owner) if act == "recv" else owner))
            def _():
                cp = cross_copy(cv, d)
                {"start": cp.start, "recv": cp.wait_recv, "send": cp.wait_send}[act]()

    def to_partner(cv, k, src, dst):
        return pltpu.make_async_remote_copy(
            src_ref=src, dst_ref=dst, send_sem=mid_send.at[cv, k], recv_sem=mid_recv.at[cv, k],
            device_id=partner, device_id_type=MESH)

    all_w, all_h = pl.ds(0, WP), pl.ds(0, HP)
    to_first = [
        to_partner(0, 0, c1_h.at[0], F1.at[1, pl.ds(1, R), pl.ds(0, W)]),
        to_partner(0, 1, F1.at[0, 0, all_w], F1.at[1, 0, all_w]),
        to_partner(0, 2, F1.at[0, R + 1, all_w], F1.at[1, R + 1, all_w]),
        to_partner(1, 0, c2_h.at[0], F2.at[1, pl.ds(1, R), pl.ds(0, W)])]
    main = pl.ds(1, HR), pl.ds(0, HW)
    to_second = [
        to_partner(0, 0, CA.at[main], CB.at[main]),
        to_partner(1, 0, F2.at[2, 1, all_w], F2.at[1, 1, all_w]),
        to_partner(1, 1, F2.at[2, R, all_w], F2.at[1, R, all_w]),
        to_partner(1, 2, F2.at[2, pl.ds(2, R - 2), all_w], F2.at[1, pl.ds(2, R - 2), all_w]),
        to_partner(0, 1, CA.at[0, all_h], CB.at[0, all_h]),
        to_partner(0, 2, CA.at[HR + 1, all_h], CB.at[HR + 1, all_h])]

    def when_first(*bodies):
        @pl.when(first)
        def _():
            for body in bodies:
                body()

    def when_second(*bodies):
        @pl.when(second)
        def _():
            for body in bodies:
                body()

    def weights(cv, frames):
        return jnp.concatenate([w[cv, a].reshape(3 * CH, 3 * CH) for a in frames], axis=0)

    def fold_taps(place, a):
        k0, k1, k2 = (w[0, a, p].astype(f32) for p in range(3))
        for parity, pair in ((0, (k0, k1 + k2)), (1, (k0 + k1, k2))):
            for b, m in enumerate(pair):
                q0, q1, q2 = m[:, :CH], m[:, CH:2 * CH], m[:, 2 * CH:]
                wu[parity, pl.ds((2 * place + b) * CH, CH)] = jnp.concatenate(
                    [q1 + q2, q0 + q1, q0, q2], axis=1).astype(bf)

    spot = lax.broadcasted_iota(jnp.int32, (8, CH), 0)

    def fold_main(z):
        after = pltpu.roll(z[:, :CH], 1, 0)
        after = jnp.concatenate([jnp.where(spot == 0, 0.0, after[:8]), after[8:]], axis=0)
        ahead = pltpu.roll(z[:, 2 * CH:], W - 1, 0)
        ahead = jnp.concatenate([ahead[:W - 8], jnp.where(spot == 7, 0.0, ahead[W - 8:])], axis=0)
        return after + z[:, CH:2 * CH] + ahead

    def fold_ring(z):
        n = z.shape[0]
        return pltpu.roll(z[:, :CH], 1, 0) + z[:, CH:2 * CH] + pltpu.roll(z[:, 2 * CH:], n - 1, 0)

    def second_main(frames, at=0, size=R):
        lhs = jnp.concatenate(
            [F2[a, pl.ds(at + p, size), pl.ds(0, W)].reshape(size * W, CH)
             for a in frames for p in range(3)], axis=1)
        z = jnp.dot(lhs, weights(1, frames), preferred_element_type=f32)
        return [fold_main(z[n * W:(n + 1) * W]) for n in range(size)]

    def own_two(at, size):
        for n, y in enumerate(second_main((0,), at, size)):
            acc2[at + n] = y

    tall = 1 + up_ok.astype(jnp.int32) + down_ok.astype(jnp.int32)
    wide = 1 + left_ok.astype(jnp.int32) + right_ok.astype(jnp.int32)
    pl.semaphore_wait(barrier, tall * wide + wide - 1)
    when_second(lambda: sides("start", ONE, tall_ds))
    sides("start", ONE, col_ds)
    cross("start", ONE, col_ds)
    when_second(to_first[0].start)
    when_first(to_second[0].start)
    sides("start", COARSE, range(8))
    cross("start", COARSE, col_ds)

    for cp in two_cp:
        cp.wait()
    own_two(0, R)
    when_first(lambda: sides("start", ONE, tall_ds))
    when_second(to_first[3].start)
    sides("start", TWO, col_ds)
    cross("start", TWO, col_ds)

    for cp in w_cp:
        cp.wait()
    fold_taps(0, 2)
    when_second(lambda: fold_taps(1, 1))

    def first_rows(frames, spans, add=False):
        lhs = jnp.concatenate(
            [jnp.concatenate([F1[a, pl.ds(at + p, n)].reshape(n * WP, CH)
                              for a in frames for p in range(3)], axis=1) for at, n in spans],
            axis=0)
        z = jnp.dot(lhs, weights(0, frames), preferred_element_type=f32)
        rows = [at + k for at, n in spans for k in range(n)]
        for k, row in enumerate(rows):
            y = fold_ring(z[k * WP:(k + 1) * WP])
            if add:
                acc1[pl.ds(row * WP, WP)] += y
            else:
                acc1[pl.ds(row * WP, WP)] = y

    def coarse(frames):
        for parity in range(2):
            lhs = jnp.concatenate(
                [ref[pl.ds(parity + b, HR)].reshape(HR * HP, CH) for ref in frames for b in range(2)],
                axis=1)
            z = jnp.dot(lhs, wu[parity, pl.ds(0, 2 * CH * len(frames))], preferred_element_type=f32)
            for i in range(HR):
                zi = z[i * HP:(i + 1) * HP]
                even = zi[:, :CH] + pltpu.roll(zi[:, 2 * CH:3 * CH], 1, 0)
                odd = zi[:, CH:2 * CH] + pltpu.roll(zi[:, 3 * CH:], HP - 1, 0)
                base = (2 * i + parity) * WP
                for at, n, to in ((0, HW, 0), (HW, EDGE // 2, W), (HP - EDGE // 2, EDGE // 2, WP - EDGE)):
                    for k, y in ((0, even), (1, odd)):
                        acc1[pl.ds(base + to + k, n, stride=2), :] += y[at:at + n]

    def act_two(row):
        y = acc1[pl.ds(row * WP, WP)] + b1[...]
        y = y / (1.0 + jnp.exp(-y))
        F2[2, 1 + row, pl.ds(0, W)] = y[:W].astype(bf)
        F2[2, 1 + row, pl.ds(W, EDGE)] = jnp.where(right_ok, y[W:W + EDGE], 0.0).astype(bf)
        F2[2, 1 + row, pl.ds(W + EDGE, EDGE)] = jnp.where(left_ok, y[W + EDGE:], 0.0).astype(bf)

    def inner(k, carry):
        act_two(1 + k)
        return carry

    def act_inside():
        lax.fori_loop(0, R - 2, inner, 0)

    inside, border = [(1, R - 2)], [(0, 1), (R - 1, 1)]
    for cp in one_cp:
        cp.wait()

    @pl.when(second)
    def _():
        sides("recv", ONE, tall_ds)
        to_first[1].start()
        to_first[2].start()
        sides("recv", ONE, col_ds)
        first_rows((0,), inside)
        first_rows((0,), border)
        sides("recv", COARSE, range(8))
        cross("recv", COARSE, col_ds)
        for i in (0, 4, 5):
            to_second[i].wait_recv()
        coarse((CA, CB))

    @pl.when(first)
    def _():
        sides("recv", ONE, col_ds)
        cross("recv", ONE, col_ds)
        to_first[0].wait_recv()
        first_rows((0, 1), inside)
        for k in range(2):
            acc1[pl.ds(k * (R - 1) * WP, WP)] = jnp.zeros((WP, CH), f32)
        sides("recv", COARSE, range(8))
        to_second[4].start()
        to_second[5].start()
        coarse((CA,))
        act_inside()
        to_second[3].start()
        sides("recv", ONE, tall_ds)
        to_first[1].wait_recv()
        to_first[2].wait_recv()
        first_rows((0, 1), border, True)

    for k in range(2):
        act_two(k * (R - 1))
    when_first(to_second[1].start, to_second[2].start)

    when_second(act_inside)

    sides("recv", TWO, col_ds)
    cross("recv", TWO, col_ds)
    when_first(to_first[3].wait_recv)
    when_second(to_second[1].wait_recv, to_second[2].wait_recv)

    def part_copy(k):
        return pltpu.make_async_remote_copy(
            src_ref=ps.at[k], dst_ref=pr.at[1 - k], send_sem=part_send.at[k],
            recv_sem=part_recv.at[1 - k], device_id={"row": r - 1 + 2 * k}, device_id_type=MESH)

    reach = (up_ok, down_ok)
    for k in range(2):
        lhs = jnp.concatenate([F2[a, 1 + k * (R - 1)] for a in range(3)], axis=1)
        rhs = jnp.concatenate([w[1, a, 2 - 2 * k] for a in range(3)], axis=0)
        ps[k] = fold_ring(jnp.dot(lhs, rhs, preferred_element_type=f32))[:W].astype(bf)
    for k in range(2):
        @pl.when(reach[k])
        def _():
            part_copy(k).start()

    when_second(to_second[3].wait_recv)
    for n, y in enumerate(second_main((1, 2))):
        acc2[n] += y

    lhs = jnp.concatenate(
        [F2[a, pl.ds(p, R), pl.ds(W, 2 * EDGE)].reshape(R * 2 * EDGE, CH)
         for a in range(3) for p in range(3)], axis=1)
    z = jnp.dot(lhs, weights(1, range(3)), preferred_element_type=f32)
    for n in range(R):
        part = z[n * 2 * EDGE:(n + 1) * 2 * EDGE]
        acc2[n, pl.ds(0, 1)] += part[2 * EDGE - 1:, :CH]
        acc2[n, pl.ds(W - 1, 1)] += part[:1, 2 * CH:]

    def finish(row):
        y = acc2[row] + b2[...] + up[row // 2].astype(f32)
        out_v[0, row] = y.astype(bf)

    def last(k, carry):
        finish(1 + k)
        return carry

    lax.fori_loop(0, R - 2, last, 0)
    for k in range(2):
        row = k * (R - 1)

        @pl.when(reach[k])
        def _():
            part_copy(1 - k).wait_recv()
            acc2[row] += pr[k].astype(f32)

        finish(row)

    for cv, ds in ((ONE, range(8)), (COARSE, range(8)), (TWO, col_ds)):
        sides("send", cv, ds)
        cross("send", cv, col_ds)
    when_second(*[cp.wait_send for cp in to_first])
    when_first(*[cp.wait_send for cp in to_second])
    for k in range(2):
        @pl.when(reach[k])
        def _():
            part_copy(k).wait_send()


def store(src, dst, sem):
    cp = pltpu.make_async_copy(src, dst, sem)
    cp.start()
    cp.wait()


def per_device(latent, proj_weight, proj_bias, cache_one, cache_two,
               conv_one, bias_one, conv_two, bias_two):
    _, R, W, CH = cache_one.shape
    _, HR, HW, LCH = latent.shape
    WP, HP = W + 2 * EDGE, HW + 2 * EDGE
    anywhere = pl.BlockSpec(memory_space=pl.ANY)
    bf, f32 = jnp.bfloat16, jnp.float32
    dma = pltpu.SemaphoreType.DMA
    decoded = pl.pallas_call(
        functools.partial(kernel, lax.axis_size("row"), lax.axis_size("col")),
        out_shape=pltpu.VMEM(cache_one.shape, bf),
        in_specs=[anywhere] * 9,
        out_specs=pl.BlockSpec(memory_space=pltpu.VMEM),
        scratch_shapes=[
            pltpu.VMEM((HR, HW, LCH), bf),
            pltpu.VMEM((LCH, CH), bf),
            pltpu.VMEM((2, 3, 3, CH, 3 * CH), bf),
            pltpu.VMEM((2, 4 * CH, 4 * CH), bf),
            pltpu.VMEM((2, R + 2, WP, CH), bf),
            pltpu.VMEM((HR + 2, HP, CH), bf),
            pltpu.VMEM((HR + 2, HP, CH), bf),
            pltpu.VMEM((3, R + 2, WP, CH), bf),
            pltpu.VMEM((HR, W, CH), bf),
            pltpu.VMEM((R * WP, CH), f32),
            pltpu.VMEM((R, W, CH), f32),
            pltpu.VMEM((W, CH), f32),
            pltpu.VMEM((2, W, CH), bf),
            pltpu.VMEM((2, W, CH), bf),
            pltpu.VMEM((1, CH), f32),
            pltpu.VMEM((1, CH), f32),
            pltpu.VMEM((1, CH), f32),
            dma((13,)), dma((3, 8)), dma((3, 8)), dma((3, 2)), dma((3, 2)),
            dma((2, 3)), dma((2, 3)), dma((2,)), dma((2,)),
        ],
        compiler_params=pltpu.CompilerParams(
            collective_id=0, has_side_effects=True, vmem_limit_bytes=60 * 1024 * 1024),
        name="decoder_window",
    )(latent, proj_weight, proj_bias.reshape(1, CH), cache_one, cache_two,
      conv_one, bias_one.reshape(1, CH), conv_two, bias_two.reshape(1, CH))
    return pl.pallas_call(
        store,
        out_shape=jax.ShapeDtypeStruct(cache_one.shape, bf),
        in_specs=[pl.BlockSpec(memory_space=pltpu.VMEM)],
        out_specs=anywhere,
        scratch_shapes=[dma],
        compiler_params=pltpu.CompilerParams(vmem_limit_bytes=1024 * 1024),
        name="store",
    )(decoded)


def solution(mesh):
    placed = P(("grp", "frm"), "row", "col", None)
    return jax.shard_map(
        per_device,
        mesh=mesh,
        in_specs=(placed, P(), P(), placed, placed, P(), P(), P(), P()),
        out_specs=placed,
        check_vma=False,
    )
```

```python
import functools

import jax
import jax.numpy as jnp
from jax import lax
from jax.experimental import pallas as pl
from jax.experimental.pallas import tpu as pltpu
from jax.sharding import PartitionSpec as P

EDGE = 16
MESH = pl.DeviceIdType.MESH
SIDES = [(-1, 0), (1, 0), (0, -1), (0, 1), (-1, -1), (-1, 1), (1, -1), (1, 1)]
ONE, COARSE, TWO = 0, 1, 2
MIDDLE = (1, 0, 1)


def kernel(rows_n, cols_n, lat_h, pw_h, pb_h, c1_h, c2_h, w1_h, b1_h, w2_h, b2_h, out_v,
           lat, pw, w, wu, F1, CA, CB, F2, up, acc1, acc2, s1, ps, pr, pb, b1, b2,
           load_sem, side_send, side_recv, cross_send, cross_recv,
           mid_send, mid_recv, part_send, part_recv):
    R, W, CH = c1_h.shape[1], c1_h.shape[2], c1_h.shape[3]
    HR, HW = lat.shape[0], lat.shape[1]
    WP, HP = W + 2 * EDGE, HW + 2 * EDGE
    bf, f32 = jnp.bfloat16, jnp.float32
    r, c, f = lax.axis_index("row"), lax.axis_index("col"), lax.axis_index("frm")
    up_ok, down_ok = r > 0, r < rows_n - 1
    left_ok, right_ok = c > 0, c < cols_n - 1
    first, second = f == 0, f == 1

    def exists(d):
        dr, dc = SIDES[d]
        ok = None
        for test in ([up_ok] if dr < 0 else [down_ok] if dr > 0 else []) + (
                [left_ok] if dc < 0 else [right_ok] if dc > 0 else []):
            ok = test if ok is None else jnp.logical_and(ok, test)
        return ok

    def where_is(d):
        dr, dc = SIDES[d]
        ids = {}
        if dr:
            ids["row"] = r + dr
        if dc:
            ids["col"] = c + dc
        return ids

    def opposite(d):
        return SIDES.index((-SIDES[d][0], -SIDES[d][1]))

    loads = []

    def load(src, dst):
        cp = pltpu.make_async_copy(src, dst, load_sem.at[len(loads)])
        cp.start()
        loads.append(cp)
        return cp

    def load_weights(cv, src):
        return [load(src.at[:, :, q], w.at[cv, :, :, :, pl.ds(q * CH, CH)]) for q in range(3)]

    first_cp = [load(lat_h.at[0], lat), load(pw_h, pw), load(pb_h, pb)]
    two_cp = [load(c2_h.at[0], F2.at[0, pl.ds(1, R), pl.ds(0, W)])] + load_weights(1, w2_h)
    w_cp = load_weights(0, w1_h)
    one_cp = [load(c1_h.at[0], F1.at[0, pl.ds(1, R), pl.ds(0, W)]), load(b1_h, b1), load(b2_h, b2)]

    partner = {"frm": 1 - f}
    barrier = pltpu.get_barrier_semaphore()
    for d in range(8):
        @pl.when(exists(d))
        def _():
            for ids in ({}, partner)[:2 if SIDES[d][0] == 0 else 1]:
                pl.semaphore_signal(barrier, inc=1, device_id={**where_is(d), **ids},
                                    device_id_type=MESH)
    pl.semaphore_signal(barrier, inc=1, device_id=partner, device_id_type=MESH)

    def clear(ref, *place):
        shape = ref.at[place].shape
        ref[place] = jnp.zeros(shape, bf)

    rims = ((left_ok, lambda n: pl.ds(n - EDGE, EDGE)), (right_ok, lambda n: pl.ds(n - 2 * EDGE, EDGE)))
    for ref, tall, wide in ((F1.at[0], R, WP), (CA, HR, HP)):
        for ok, row in ((up_ok, 0), (down_ok, tall + 1)):
            @pl.when(jnp.logical_not(ok))
            def _():
                clear(ref, row, pl.ds(0, wide))
        for ok, rim in rims:
            @pl.when(jnp.logical_not(ok))
            def _():
                clear(ref, pl.ds(0, tall + 2), rim(wide))
    for ok, rim in rims:
        @pl.when(jnp.logical_not(ok))
        def _():
            clear(F2, 0, pl.ds(1, R), rim(WP))

            @pl.when(first)
            def _():
                clear(F1, 1, pl.ds(1, R), rim(WP))
                clear(F2, 1, pl.ds(1, R), rim(WP))

            @pl.when(second)
            def _():
                clear(CB, pl.ds(1, HR), rim(HP))
    for a in range(3):
        for row in (0, R + 1):
            clear(F2, a, row, pl.ds(0, WP))

    for cp in first_cp:
        cp.wait()

    def project(i, carry):
        v = jnp.dot(lat[i], pw[...], preferred_element_type=f32) + pb[...]
        v = v.astype(bf).astype(f32)
        CA[1 + i, pl.ds(0, HW)] = (v / (1.0 + jnp.exp(-v))).astype(bf)
        for k in range(2):
            s1[pl.ds(k, HW, stride=2), :] = v
        up[i] = s1[...].astype(bf)
        return carry

    lax.fori_loop(0, HR, project, 0)

    def side_refs(cv, d, slot=0):
        dr, dc = SIDES[d]
        n, m = (HR, HW) if cv == COARSE else (R, W)
        row, land_row = (0, n + 1) if dr < 0 else (n - 1, 0)
        col, land_col = ((0, m) if dc < 0 else (m - EDGE, m + EDGE))
        rows, land_rows = (pl.ds(row, 1), pl.ds(land_row, 1)) if dr else (pl.ds(0, n), pl.ds(1, n))
        cols, land_cols = (
            (pl.ds(col, EDGE), pl.ds(land_col, EDGE)) if dc else (pl.ds(0, m), pl.ds(0, m)))
        if cv == COARSE:
            src = CA.at[pl.ds(1 + rows.start, rows.size), cols]
            return src, (CB if slot else CA).at[land_rows, land_cols]
        src = (c1_h, c2_h)[cv // 2].at[0, rows, cols]
        return src, (F1, F2)[cv // 2].at[slot, land_rows, land_cols]

    def side_copy(cv, d):
        src, dst = side_refs(cv, d)
        return pltpu.make_async_remote_copy(
            src_ref=src, dst_ref=dst, send_sem=side_send.at[cv, d], recv_sem=side_recv.at[cv, d],
            device_id=where_is(d), device_id_type=MESH)

    def cross_copy(cv, d):
        src, dst = side_refs(cv, d, 1)
        return pltpu.make_async_remote_copy(
            src_ref=src, dst_ref=dst, send_sem=cross_send.at[cv, d - 2],
            recv_sem=cross_recv.at[cv, d - 2], device_id={**where_is(d), **partner},
            device_id_type=MESH)

    tall_ds, col_ds = (0, 1, 4, 5, 6, 7), (2, 3)

    def sides(act, cv, ds):
        for d in ds:
            @pl.when(exists(opposite(d) if act == "recv" else d))
            def _():
                cp = side_copy(cv, d)
                {"start": cp.start, "recv": cp.wait_recv, "send": cp.wait_send}[act]()

    def cross(act, cv, ds):
        owner = f == MIDDLE[cv]
        for d in ds:
            there = exists(opposite(d) if act == "recv" else d)

            @pl.when(jnp.logical_and(there, jnp.logical_not(owner) if act == "recv" else owner))
            def _():
                cp = cross_copy(cv, d)
                {"start": cp.start, "recv": cp.wait_recv, "send": cp.wait_send}[act]()

    def to_partner(cv, k, src, dst):
        return pltpu.make_async_remote_copy(
            src_ref=src, dst_ref=dst, send_sem=mid_send.at[cv, k], recv_sem=mid_recv.at[cv, k],
            device_id=partner, device_id_type=MESH)

    all_w, all_h = pl.ds(0, WP), pl.ds(0, HP)
    to_first = [
        to_partner(0, 0, c1_h.at[0], F1.at[1, pl.ds(1, R), pl.ds(0, W)]),
        to_partner(0, 1, F1.at[0, 0, all_w], F1.at[1, 0, all_w]),
        to_partner(0, 2, F1.at[0, R + 1, all_w], F1.at[1, R + 1, all_w]),
        to_partner(1, 0, c2_h.at[0], F2.at[1, pl.ds(1, R), pl.ds(0, W)])]
    main = pl.ds(1, HR), pl.ds(0, HW)
    to_second = [
        to_partner(0, 0, CA.at[main], CB.at[main]),
        to_partner(1, 0, F2.at[2, 1, all_w], F2.at[1, 1, all_w]),
        to_partner(1, 1, F2.at[2, R, all_w], F2.at[1, R, all_w]),
        to_partner(1, 2, F2.at[2, pl.ds(2, R - 2), all_w], F2.at[1, pl.ds(2, R - 2), all_w]),
        to_partner(0, 1, CA.at[0, all_h], CB.at[0, all_h]),
        to_partner(0, 2, CA.at[HR + 1, all_h], CB.at[HR + 1, all_h])]

    def when_first(*bodies):
        @pl.when(first)
        def _():
            for body in bodies:
                body()

    def when_second(*bodies):
        @pl.when(second)
        def _():
            for body in bodies:
                body()

    def weights(cv, frames):
        return jnp.concatenate([w[cv, a].reshape(3 * CH, 3 * CH) for a in frames], axis=0)

    def fold_taps(place, a):
        k0, k1, k2 = (w[0, a, p].astype(f32) for p in range(3))
        for parity, pair in ((0, (k0, k1 + k2)), (1, (k0 + k1, k2))):
            for b, m in enumerate(pair):
                q0, q1, q2 = m[:, :CH], m[:, CH:2 * CH], m[:, 2 * CH:]
                wu[parity, pl.ds((2 * place + b) * CH, CH)] = jnp.concatenate(
                    [q1 + q2, q0 + q1, q0, q2], axis=1).astype(bf)

    spot = lax.broadcasted_iota(jnp.int32, (8, CH), 0)

    def fold_main(z):
        after = pltpu.roll(z[:, :CH], 1, 0)
        after = jnp.concatenate([jnp.where(spot == 0, 0.0, after[:8]), after[8:]], axis=0)
        ahead = pltpu.roll(z[:, 2 * CH:], W - 1, 0)
        ahead = jnp.concatenate([ahead[:W - 8], jnp.where(spot == 7, 0.0, ahead[W - 8:])], axis=0)
        return after + z[:, CH:2 * CH] + ahead

    def fold_ring(z):
        n = z.shape[0]
        return pltpu.roll(z[:, :CH], 1, 0) + z[:, CH:2 * CH] + pltpu.roll(z[:, 2 * CH:], n - 1, 0)

    def second_main(frames, at=0, size=R):
        lhs = jnp.concatenate(
            [F2[a, pl.ds(at + p, size), pl.ds(0, W)].reshape(size * W, CH)
             for a in frames for p in range(3)], axis=1)
        z = jnp.dot(lhs, weights(1, frames), preferred_element_type=f32)
        return [fold_main(z[n * W:(n + 1) * W]) for n in range(size)]

    def own_two(at, size):
        for n, y in enumerate(second_main((0,), at, size)):
            acc2[at + n] = y

    tall = 1 + up_ok.astype(jnp.int32) + down_ok.astype(jnp.int32)
    wide = 1 + left_ok.astype(jnp.int32) + right_ok.astype(jnp.int32)
    pl.semaphore_wait(barrier, tall * wide + wide - 1)
    when_second(lambda: sides("start", ONE, tall_ds))
    sides("start", ONE, col_ds)
    cross("start", ONE, col_ds)
    when_second(to_first[0].start)
    when_first(to_second[0].start)
    sides("start", COARSE, range(8))
    cross("start", COARSE, col_ds)
    when_first(lambda: sides("start", ONE, tall_ds))

    for cp in two_cp:
        cp.wait()
    own_two(0, R)
    when_second(to_first[3].start)
    sides("start", TWO, col_ds)
    cross("start", TWO, col_ds)

    for cp in w_cp:
        cp.wait()
    fold_taps(0, 2)
    when_second(lambda: fold_taps(1, 1))

    def inside_dot(frames, at, n):
        lhs = jnp.concatenate(
            [F1[a, pl.ds(1 + p, R - 2), pl.ds(at, n)].reshape((R - 2) * n, CH)
             for a in frames for p in range(3)], axis=1)
        z = jnp.dot(lhs, weights(0, frames), preferred_element_type=f32)
        return [z[k * n:(k + 1) * n] for k in range(R - 2)]

    def inside_main(frames):
        for k, z in enumerate(inside_dot(frames, 0, W)):
            z = jnp.concatenate([z, jnp.zeros((2 * EDGE, 3 * CH), f32)], axis=0)
            acc1[pl.ds((1 + k) * WP, WP)] = fold_ring(z)

    def inside_rim(frames):
        rest = jnp.zeros((EDGE, 3 * CH), f32)
        for k, z in enumerate(inside_dot(frames, W, 2 * EDGE)):
            y = fold_ring(jnp.concatenate([rest, z, rest], axis=0))
            acc1[pl.ds((1 + k) * WP + W - EDGE, 3 * EDGE)] += y[:3 * EDGE]
            acc1[pl.ds((1 + k) * WP, EDGE)] += y[3 * EDGE:]

    def border_line(k):
        return pl.ds(k * (R - 1) * WP, WP)

    def border_dot(frames, rows, taps):
        lhs = jnp.concatenate([F1[a, row] for a in frames for row in rows], axis=1)
        rhs = jnp.concatenate([w[0, a, p] for a in frames for p in taps], axis=0)
        return fold_ring(jnp.dot(lhs, rhs, preferred_element_type=f32))

    def border_own(frames):
        for k in range(2):
            acc1[border_line(k)] = border_dot(frames, ((1, 2), (R - 1, R))[k], ((1, 2), (0, 1))[k])

    def border_halo(frames):
        for k in range(2):
            acc1[border_line(k)] += border_dot(frames, (k * (R + 1),), (2 * k,))

    def coarse(frames):
        for parity in range(2):
            lhs = jnp.concatenate(
                [ref[pl.ds(parity + b, HR)].reshape(HR * HP, CH) for ref in frames for b in range(2)],
                axis=1)
            z = jnp.dot(lhs, wu[parity, pl.ds(0, 2 * CH * len(frames))], preferred_element_type=f32)
            for i in range(HR):
                zi = z[i * HP:(i + 1) * HP]
                even = zi[:, :CH] + pltpu.roll(zi[:, 2 * CH:3 * CH], 1, 0)
                odd = zi[:, CH:2 * CH] + pltpu.roll(zi[:, 3 * CH:], HP - 1, 0)
                base = (2 * i + parity) * WP
                for at, n, to in ((0, HW, 0), (HW, EDGE // 2, W), (HP - EDGE // 2, EDGE // 2, WP - EDGE)):
                    for k, y in ((0, even), (1, odd)):
                        acc1[pl.ds(base + to + k, n, stride=2), :] += y[at:at + n]

    def act_two(row):
        y = acc1[pl.ds(row * WP, WP)] + b1[...]
        y = y / (1.0 + jnp.exp(-y))
        F2[2, 1 + row, pl.ds(0, W)] = y[:W].astype(bf)
        F2[2, 1 + row, pl.ds(W, EDGE)] = jnp.where(right_ok, y[W:W + EDGE], 0.0).astype(bf)
        F2[2, 1 + row, pl.ds(W + EDGE, EDGE)] = jnp.where(left_ok, y[W + EDGE:], 0.0).astype(bf)

    def inner(k, carry):
        act_two(1 + k)
        return carry

    def act_inside():
        lax.fori_loop(0, R - 2, inner, 0)

    for cp in one_cp:
        cp.wait()

    @pl.when(second)
    def _():
        inside_main((0,))
        sides("recv", ONE, tall_ds)
        to_first[1].start()
        to_first[2].start()
        sides("recv", ONE, col_ds)
        inside_rim((0,))
        border_own((0,))
        border_halo((0,))
        sides("recv", COARSE, range(8))
        cross("recv", COARSE, col_ds)
        for i in (0, 4, 5):
            to_second[i].wait_recv()
        coarse((CA, CB))

    @pl.when(first)
    def _():
        to_first[0].wait_recv()
        inside_main((0, 1))
        sides("recv", ONE, col_ds)
        cross("recv", ONE, col_ds)
        inside_rim((0, 1))
        border_own((0, 1))
        sides("recv", COARSE, range(8))
        to_second[4].start()
        to_second[5].start()
        coarse((CA,))
        act_inside()
        to_second[3].start()
        sides("recv", ONE, tall_ds)
        to_first[1].wait_recv()
        to_first[2].wait_recv()
        border_halo((0, 1))

    for k in range(2):
        act_two(k * (R - 1))
    when_first(to_second[1].start, to_second[2].start)

    when_second(act_inside)

    sides("recv", TWO, col_ds)
    cross("recv", TWO, col_ds)
    when_first(to_first[3].wait_recv)
    when_second(to_second[1].wait_recv, to_second[2].wait_recv)

    def part_copy(k):
        return pltpu.make_async_remote_copy(
            src_ref=ps.at[k], dst_ref=pr.at[1 - k], send_sem=part_send.at[k],
            recv_sem=part_recv.at[1 - k], device_id={"row": r - 1 + 2 * k}, device_id_type=MESH)

    reach = (up_ok, down_ok)
    for k in range(2):
        lhs = jnp.concatenate([F2[a, 1 + k * (R - 1)] for a in range(3)], axis=1)
        rhs = jnp.concatenate([w[1, a, 2 - 2 * k] for a in range(3)], axis=0)
        ps[k] = fold_ring(jnp.dot(lhs, rhs, preferred_element_type=f32))[:W].astype(bf)
    for k in range(2):
        @pl.when(reach[k])
        def _():
            part_copy(k).start()

    when_second(to_second[3].wait_recv)
    for n, y in enumerate(second_main((1, 2))):
        acc2[n] += y

    lhs = jnp.concatenate(
        [F2[a, pl.ds(p, R), pl.ds(W, 2 * EDGE)].reshape(R * 2 * EDGE, CH)
         for a in range(3) for p in range(3)], axis=1)
    z = jnp.dot(lhs, weights(1, range(3)), preferred_element_type=f32)
    for n in range(R):
        part = z[n * 2 * EDGE:(n + 1) * 2 * EDGE]
        acc2[n, pl.ds(0, 1)] += part[2 * EDGE - 1:, :CH]
        acc2[n, pl.ds(W - 1, 1)] += part[:1, 2 * CH:]

    def finish(row):
        y = acc2[row] + b2[...] + up[row // 2].astype(f32)
        out_v[0, row] = y.astype(bf)

    def last(k, carry):
        finish(1 + k)
        return carry

    lax.fori_loop(0, R - 2, last, 0)
    for k in range(2):
        row = k * (R - 1)

        @pl.when(reach[k])
        def _():
            part_copy(1 - k).wait_recv()
            acc2[row] += pr[k].astype(f32)

        finish(row)

    for cv, ds in ((ONE, range(8)), (COARSE, range(8)), (TWO, col_ds)):
        sides("send", cv, ds)
        cross("send", cv, col_ds)
    when_second(*[cp.wait_send for cp in to_first])
    when_first(*[cp.wait_send for cp in to_second])
    for k in range(2):
        @pl.when(reach[k])
        def _():
            part_copy(k).wait_send()


def store(src, dst, sem):
    cp = pltpu.make_async_copy(src, dst, sem)
    cp.start()
    cp.wait()


def per_device(latent, proj_weight, proj_bias, cache_one, cache_two,
               conv_one, bias_one, conv_two, bias_two):
    _, R, W, CH = cache_one.shape
    _, HR, HW, LCH = latent.shape
    WP, HP = W + 2 * EDGE, HW + 2 * EDGE
    anywhere = pl.BlockSpec(memory_space=pl.ANY)
    bf, f32 = jnp.bfloat16, jnp.float32
    dma = pltpu.SemaphoreType.DMA
    decoded = pl.pallas_call(
        functools.partial(kernel, lax.axis_size("row"), lax.axis_size("col")),
        out_shape=pltpu.VMEM(cache_one.shape, bf),
        in_specs=[anywhere] * 9,
        out_specs=pl.BlockSpec(memory_space=pltpu.VMEM),
        scratch_shapes=[
            pltpu.VMEM((HR, HW, LCH), bf),
            pltpu.VMEM((LCH, CH), bf),
            pltpu.VMEM((2, 3, 3, CH, 3 * CH), bf),
            pltpu.VMEM((2, 4 * CH, 4 * CH), bf),
            pltpu.VMEM((2, R + 2, WP, CH), bf),
            pltpu.VMEM((HR + 2, HP, CH), bf),
            pltpu.VMEM((HR + 2, HP, CH), bf),
            pltpu.VMEM((3, R + 2, WP, CH), bf),
            pltpu.VMEM((HR, W, CH), bf),
            pltpu.VMEM((R * WP, CH), f32),
            pltpu.VMEM((R, W, CH), f32),
            pltpu.VMEM((W, CH), f32),
            pltpu.VMEM((2, W, CH), bf),
            pltpu.VMEM((2, W, CH), bf),
            pltpu.VMEM((1, CH), f32),
            pltpu.VMEM((1, CH), f32),
            pltpu.VMEM((1, CH), f32),
            dma((13,)), dma((3, 8)), dma((3, 8)), dma((3, 2)), dma((3, 2)),
            dma((2, 3)), dma((2, 3)), dma((2,)), dma((2,)),
        ],
        compiler_params=pltpu.CompilerParams(
            collective_id=0, has_side_effects=True, vmem_limit_bytes=60 * 1024 * 1024),
        name="decoder_window",
    )(latent, proj_weight, proj_bias.reshape(1, CH), cache_one, cache_two,
      conv_one, bias_one.reshape(1, CH), conv_two, bias_two.reshape(1, CH))
    return pl.pallas_call(
        store,
        out_shape=jax.ShapeDtypeStruct(cache_one.shape, bf),
        in_specs=[pl.BlockSpec(memory_space=pltpu.VMEM)],
        out_specs=anywhere,
        scratch_shapes=[dma],
        compiler_params=pltpu.CompilerParams(vmem_limit_bytes=1024 * 1024),
        name="store",
    )(decoded)


def solution(mesh):
    placed = P(("grp", "frm"), "row", "col", None)
    return jax.shard_map(
        per_device,
        mesh=mesh,
        in_specs=(placed, P(), P(), placed, placed, P(), P(), P(), P()),
        out_specs=placed,
        check_vma=False,
    )
```

```python
import functools

import jax
import jax.numpy as jnp
from jax import lax
from jax.experimental import pallas as pl
from jax.experimental.pallas import tpu as pltpu
from jax.sharding import PartitionSpec as P

EDGE = 16
MESH = pl.DeviceIdType.MESH
SIDES = [(-1, 0), (1, 0), (0, -1), (0, 1), (-1, -1), (-1, 1), (1, -1), (1, 1)]
ONE, COARSE, TWO = 0, 1, 2
MIDDLE = (1, 0, 1)


def kernel(rows_n, cols_n, lat_h, pw_h, pb_h, c1_h, c2_h, w1_h, b1_h, w2_h, b2_h, out_v,
           lat, pw, w, wu, F1, CA, CB, F2, up, acc1, acc2, s1, ps, pr, pb, b1, b2,
           load_sem, side_send, side_recv, cross_send, cross_recv,
           mid_send, mid_recv, part_send, part_recv):
    R, W, CH = c1_h.shape[1], c1_h.shape[2], c1_h.shape[3]
    HR, HW = lat.shape[0], lat.shape[1]
    WP, HP = W + 2 * EDGE, HW + 2 * EDGE
    bf, f32 = jnp.bfloat16, jnp.float32
    r, c, f = lax.axis_index("row"), lax.axis_index("col"), lax.axis_index("frm")
    up_ok, down_ok = r > 0, r < rows_n - 1
    left_ok, right_ok = c > 0, c < cols_n - 1
    first, second = f == 0, f == 1

    def exists(d):
        dr, dc = SIDES[d]
        ok = None
        for test in ([up_ok] if dr < 0 else [down_ok] if dr > 0 else []) + (
                [left_ok] if dc < 0 else [right_ok] if dc > 0 else []):
            ok = test if ok is None else jnp.logical_and(ok, test)
        return ok

    def where_is(d):
        dr, dc = SIDES[d]
        ids = {}
        if dr:
            ids["row"] = r + dr
        if dc:
            ids["col"] = c + dc
        return ids

    def opposite(d):
        return SIDES.index((-SIDES[d][0], -SIDES[d][1]))

    loads = []

    def load(src, dst):
        cp = pltpu.make_async_copy(src, dst, load_sem.at[len(loads)])
        cp.start()
        loads.append(cp)
        return cp

    def load_weights(cv, src):
        return [load(src.at[:, :, q], w.at[cv, :, :, :, pl.ds(q * CH, CH)]) for q in range(3)]

    first_cp = [load(lat_h.at[0], lat), load(pw_h, pw), load(pb_h, pb)]
    two_cp = [load(c2_h.at[0], F2.at[0, pl.ds(1, R), pl.ds(0, W)])] + load_weights(1, w2_h)
    w_cp = load_weights(0, w1_h)
    one_cp = [load(c1_h.at[0], F1.at[0, pl.ds(1, R), pl.ds(0, W)]), load(b1_h, b1), load(b2_h, b2)]

    partner = {"frm": 1 - f}
    barrier = pltpu.get_barrier_semaphore()
    for d in range(8):
        @pl.when(exists(d))
        def _():
            for ids in ({}, partner)[:2 if SIDES[d][0] == 0 else 1]:
                pl.semaphore_signal(barrier, inc=1, device_id={**where_is(d), **ids},
                                    device_id_type=MESH)
    pl.semaphore_signal(barrier, inc=1, device_id=partner, device_id_type=MESH)

    def clear(ref, *place):
        shape = ref.at[place].shape
        ref[place] = jnp.zeros(shape, bf)

    rims = ((left_ok, lambda n: pl.ds(n - EDGE, EDGE)), (right_ok, lambda n: pl.ds(n - 2 * EDGE, EDGE)))
    for ref, tall, wide in ((F1.at[0], R, WP), (CA, HR, HP)):
        for ok, row in ((up_ok, 0), (down_ok, tall + 1)):
            @pl.when(jnp.logical_not(ok))
            def _():
                clear(ref, row, pl.ds(0, wide))
        for ok, rim in rims:
            @pl.when(jnp.logical_not(ok))
            def _():
                clear(ref, pl.ds(0, tall + 2), rim(wide))
    for ok, rim in rims:
        @pl.when(jnp.logical_not(ok))
        def _():
            clear(F2, 0, pl.ds(1, R), rim(WP))

            @pl.when(first)
            def _():
                clear(F1, 1, pl.ds(1, R), rim(WP))
                clear(F2, 1, pl.ds(1, R), rim(WP))

            @pl.when(second)
            def _():
                clear(CB, pl.ds(1, HR), rim(HP))
    for a in range(3):
        for row in (0, R + 1):
            clear(F2, a, row, pl.ds(0, WP))

    for cp in first_cp:
        cp.wait()

    def project(i, carry):
        v = jnp.dot(lat[i], pw[...], preferred_element_type=f32) + pb[...]
        v = v.astype(bf).astype(f32)
        CA[1 + i, pl.ds(0, HW)] = (v / (1.0 + jnp.exp(-v))).astype(bf)
        for k in range(2):
            s1[pl.ds(k, HW, stride=2), :] = v
        up[i] = s1[...].astype(bf)
        return carry

    lax.fori_loop(0, HR, project, 0)

    def side_refs(cv, d, slot=0):
        dr, dc = SIDES[d]
        n, m = (HR, HW) if cv == COARSE else (R, W)
        row, land_row = (0, n + 1) if dr < 0 else (n - 1, 0)
        col, land_col = ((0, m) if dc < 0 else (m - EDGE, m + EDGE))
        rows, land_rows = (pl.ds(row, 1), pl.ds(land_row, 1)) if dr else (pl.ds(0, n), pl.ds(1, n))
        cols, land_cols = (
            (pl.ds(col, EDGE), pl.ds(land_col, EDGE)) if dc else (pl.ds(0, m), pl.ds(0, m)))
        if cv == COARSE:
            src = CA.at[pl.ds(1 + rows.start, rows.size), cols]
            return src, (CB if slot else CA).at[land_rows, land_cols]
        src = (c1_h, c2_h)[cv // 2].at[0, rows, cols]
        return src, (F1, F2)[cv // 2].at[slot, land_rows, land_cols]

    def side_copy(cv, d):
        src, dst = side_refs(cv, d)
        return pltpu.make_async_remote_copy(
            src_ref=src, dst_ref=dst, send_sem=side_send.at[cv, d], recv_sem=side_recv.at[cv, d],
            device_id=where_is(d), device_id_type=MESH)

    def cross_copy(cv, d):
        src, dst = side_refs(cv, d, 1)
        return pltpu.make_async_remote_copy(
            src_ref=src, dst_ref=dst, send_sem=cross_send.at[cv, d - 2],
            recv_sem=cross_recv.at[cv, d - 2], device_id={**where_is(d), **partner},
            device_id_type=MESH)

    tall_ds, col_ds = (0, 1, 4, 5, 6, 7), (2, 3)

    def sides(act, cv, ds):
        for d in ds:
            @pl.when(exists(opposite(d) if act == "recv" else d))
            def _():
                cp = side_copy(cv, d)
                {"start": cp.start, "recv": cp.wait_recv, "send": cp.wait_send}[act]()

    def cross(act, cv, ds):
        owner = f == MIDDLE[cv]
        for d in ds:
            there = exists(opposite(d) if act == "recv" else d)

            @pl.when(jnp.logical_and(there, jnp.logical_not(owner) if act == "recv" else owner))
            def _():
                cp = cross_copy(cv, d)
                {"start": cp.start, "recv": cp.wait_recv, "send": cp.wait_send}[act]()

    def to_partner(cv, k, src, dst):
        return pltpu.make_async_remote_copy(
            src_ref=src, dst_ref=dst, send_sem=mid_send.at[cv, k], recv_sem=mid_recv.at[cv, k],
            device_id=partner, device_id_type=MESH)

    all_w, all_h = pl.ds(0, WP), pl.ds(0, HP)
    to_first = [
        to_partner(0, 0, c1_h.at[0], F1.at[1, pl.ds(1, R), pl.ds(0, W)]),
        to_partner(0, 1, F1.at[0, 0, all_w], F1.at[1, 0, all_w]),
        to_partner(0, 2, F1.at[0, R + 1, all_w], F1.at[1, R + 1, all_w]),
        to_partner(1, 0, c2_h.at[0], F2.at[1, pl.ds(1, R), pl.ds(0, W)])]
    main = pl.ds(1, HR), pl.ds(0, HW)
    to_second = [
        to_partner(0, 0, CA.at[main], CB.at[main]),
        to_partner(1, 0, F2.at[2, 1, all_w], F2.at[1, 1, all_w]),
        to_partner(1, 1, F2.at[2, R, all_w], F2.at[1, R, all_w]),
        to_partner(1, 2, F2.at[2, pl.ds(2, R - 2), all_w], F2.at[1, pl.ds(2, R - 2), all_w]),
        to_partner(0, 1, CA.at[0, all_h], CB.at[0, all_h]),
        to_partner(0, 2, CA.at[HR + 1, all_h], CB.at[HR + 1, all_h])]

    def when_first(*bodies):
        @pl.when(first)
        def _():
            for body in bodies:
                body()

    def when_second(*bodies):
        @pl.when(second)
        def _():
            for body in bodies:
                body()

    def weights(cv, frames):
        return jnp.concatenate([w[cv, a].reshape(3 * CH, 3 * CH) for a in frames], axis=0)

    def fold_taps(place, a):
        k0, k1, k2 = (w[0, a, p].astype(f32) for p in range(3))
        for parity, pair in ((0, (k0, k1 + k2)), (1, (k0 + k1, k2))):
            for b, m in enumerate(pair):
                q0, q1, q2 = m[:, :CH], m[:, CH:2 * CH], m[:, 2 * CH:]
                wu[parity, pl.ds((2 * place + b) * CH, CH)] = jnp.concatenate(
                    [q1 + q2, q0 + q1, q0, q2], axis=1).astype(bf)

    spot = lax.broadcasted_iota(jnp.int32, (8, CH), 0)

    def fold_main(z):
        after = pltpu.roll(z[:, :CH], 1, 0)
        after = jnp.concatenate([jnp.where(spot == 0, 0.0, after[:8]), after[8:]], axis=0)
        ahead = pltpu.roll(z[:, 2 * CH:], W - 1, 0)
        ahead = jnp.concatenate([ahead[:W - 8], jnp.where(spot == 7, 0.0, ahead[W - 8:])], axis=0)
        return after + z[:, CH:2 * CH] + ahead

    def fold_ring(z):
        n = z.shape[0]
        return pltpu.roll(z[:, :CH], 1, 0) + z[:, CH:2 * CH] + pltpu.roll(z[:, 2 * CH:], n - 1, 0)

    def second_main(frames, at=0, size=R):
        lhs = jnp.concatenate(
            [F2[a, pl.ds(at + p, size), pl.ds(0, W)].reshape(size * W, CH)
             for a in frames for p in range(3)], axis=1)
        z = jnp.dot(lhs, weights(1, frames), preferred_element_type=f32)
        return [fold_main(z[n * W:(n + 1) * W]) for n in range(size)]

    def own_two(at, size):
        for n, y in enumerate(second_main((0,), at, size)):
            acc2[at + n] = y

    tall = 1 + up_ok.astype(jnp.int32) + down_ok.astype(jnp.int32)
    wide = 1 + left_ok.astype(jnp.int32) + right_ok.astype(jnp.int32)
    pl.semaphore_wait(barrier, tall * wide + wide - 1)
    sides("start", ONE, (4, 5, 6, 7))
    sides("start", COARSE, (4, 5, 6, 7))
    when_second(lambda: sides("start", ONE, (0, 1)))
    sides("start", ONE, col_ds)
    cross("start", ONE, col_ds)
    when_second(to_first[0].start)
    when_first(to_second[0].start)
    sides("start", COARSE, (0, 1, 2, 3))
    cross("start", COARSE, col_ds)
    when_first(lambda: sides("start", ONE, (0, 1)))

    for cp in two_cp:
        cp.wait()
    own_two(0, R)
    when_second(to_first[3].start)
    sides("start", TWO, col_ds)
    cross("start", TWO, col_ds)

    for cp in w_cp:
        cp.wait()
    fold_taps(0, 2)
    when_second(lambda: fold_taps(1, 1))

    def inside_dot(frames, at, n):
        lhs = jnp.concatenate(
            [F1[a, pl.ds(1 + p, R - 2), pl.ds(at, n)].reshape((R - 2) * n, CH)
             for a in frames for p in range(3)], axis=1)
        z = jnp.dot(lhs, weights(0, frames), preferred_element_type=f32)
        return [z[k * n:(k + 1) * n] for k in range(R - 2)]

    def inside_main(frames):
        for k, z in enumerate(inside_dot(frames, 0, W)):
            z = jnp.concatenate([z, jnp.zeros((2 * EDGE, 3 * CH), f32)], axis=0)
            acc1[pl.ds((1 + k) * WP, WP)] = fold_ring(z)

    def inside_rim(frames):
        rest = jnp.zeros((EDGE, 3 * CH), f32)
        for k, z in enumerate(inside_dot(frames, W, 2 * EDGE)):
            y = fold_ring(jnp.concatenate([rest, z, rest], axis=0))
            acc1[pl.ds((1 + k) * WP + W - EDGE, 3 * EDGE)] += y[:3 * EDGE]
            acc1[pl.ds((1 + k) * WP, EDGE)] += y[3 * EDGE:]

    def border_line(k):
        return pl.ds(k * (R - 1) * WP, WP)

    def border_dot(frames, rows, taps):
        lhs = jnp.concatenate([F1[a, row] for a in frames for row in rows], axis=1)
        rhs = jnp.concatenate([w[0, a, p] for a in frames for p in taps], axis=0)
        return fold_ring(jnp.dot(lhs, rhs, preferred_element_type=f32))

    def border_own(frames):
        for k in range(2):
            acc1[border_line(k)] = border_dot(frames, ((1, 2), (R - 1, R))[k], ((1, 2), (0, 1))[k])

    def border_halo(frames):
        for k in range(2):
            acc1[border_line(k)] += border_dot(frames, (k * (R + 1),), (2 * k,))

    def coarse(frames):
        for parity in range(2):
            lhs = jnp.concatenate(
                [ref[pl.ds(parity + b, HR)].reshape(HR * HP, CH) for ref in frames for b in range(2)],
                axis=1)
            z = jnp.dot(lhs, wu[parity, pl.ds(0, 2 * CH * len(frames))], preferred_element_type=f32)
            for i in range(HR):
                zi = z[i * HP:(i + 1) * HP]
                even = zi[:, :CH] + pltpu.roll(zi[:, 2 * CH:3 * CH], 1, 0)
                odd = zi[:, CH:2 * CH] + pltpu.roll(zi[:, 3 * CH:], HP - 1, 0)
                base = (2 * i + parity) * WP
                for at, n, to in ((0, HW, 0), (HW, EDGE // 2, W), (HP - EDGE // 2, EDGE // 2, WP - EDGE)):
                    for k, y in ((0, even), (1, odd)):
                        acc1[pl.ds(base + to + k, n, stride=2), :] += y[at:at + n]

    def act_two(row):
        y = acc1[pl.ds(row * WP, WP)] + b1[...]
        y = y / (1.0 + jnp.exp(-y))
        F2[2, 1 + row, pl.ds(0, W)] = y[:W].astype(bf)
        F2[2, 1 + row, pl.ds(W, EDGE)] = jnp.where(right_ok, y[W:W + EDGE], 0.0).astype(bf)
        F2[2, 1 + row, pl.ds(W + EDGE, EDGE)] = jnp.where(left_ok, y[W + EDGE:], 0.0).astype(bf)

    def inner(k, carry):
        act_two(1 + k)
        return carry

    def act_inside():
        lax.fori_loop(0, R - 2, inner, 0)

    for cp in one_cp:
        cp.wait()

    @pl.when(second)
    def _():
        inside_main((0,))
        sides("recv", ONE, tall_ds)
        to_first[1].start()
        to_first[2].start()
        sides("recv", ONE, col_ds)
        inside_rim((0,))
        border_own((0,))
        border_halo((0,))
        sides("recv", COARSE, range(8))
        cross("recv", COARSE, col_ds)
        for i in (0, 4, 5):
            to_second[i].wait_recv()
        coarse((CA, CB))

    @pl.when(first)
    def _():
        to_first[0].wait_recv()
        inside_main((0, 1))
        sides("recv", ONE, col_ds)
        cross("recv", ONE, col_ds)
        inside_rim((0, 1))
        border_own((0, 1))
        sides("recv", COARSE, range(8))
        to_second[4].start()
        to_second[5].start()
        coarse((CA,))
        act_inside()
        to_second[3].start()
        sides("recv", ONE, tall_ds)
        to_first[1].wait_recv()
        to_first[2].wait_recv()
        border_halo((0, 1))

    for k in range(2):
        act_two(k * (R - 1))
    when_first(to_second[1].start, to_second[2].start)

    when_second(act_inside)

    sides("recv", TWO, col_ds)
    cross("recv", TWO, col_ds)
    when_first(to_first[3].wait_recv)
    when_second(to_second[1].wait_recv, to_second[2].wait_recv)

    def part_copy(k):
        return pltpu.make_async_remote_copy(
            src_ref=ps.at[k], dst_ref=pr.at[1 - k], send_sem=part_send.at[k],
            recv_sem=part_recv.at[1 - k], device_id={"row": r - 1 + 2 * k}, device_id_type=MESH)

    reach = (up_ok, down_ok)
    for k in range(2):
        lhs = jnp.concatenate([F2[a, 1 + k * (R - 1)] for a in range(3)], axis=1)
        rhs = jnp.concatenate([w[1, a, 2 - 2 * k] for a in range(3)], axis=0)
        ps[k] = fold_ring(jnp.dot(lhs, rhs, preferred_element_type=f32))[:W].astype(bf)
    for k in range(2):
        @pl.when(reach[k])
        def _():
            part_copy(k).start()

    when_second(to_second[3].wait_recv)
    for n, y in enumerate(second_main((1, 2))):
        acc2[n] += y

    lhs = jnp.concatenate(
        [F2[a, pl.ds(p, R), pl.ds(W, 2 * EDGE)].reshape(R * 2 * EDGE, CH)
         for a in range(3) for p in range(3)], axis=1)
    z = jnp.dot(lhs, weights(1, range(3)), preferred_element_type=f32)
    for n in range(R):
        part = z[n * 2 * EDGE:(n + 1) * 2 * EDGE]
        acc2[n, pl.ds(0, 1)] += part[2 * EDGE - 1:, :CH]
        acc2[n, pl.ds(W - 1, 1)] += part[:1, 2 * CH:]

    def finish(row):
        y = acc2[row] + b2[...] + up[row // 2].astype(f32)
        out_v[0, row] = y.astype(bf)

    def last(k, carry):
        finish(1 + k)
        return carry

    lax.fori_loop(0, R - 2, last, 0)
    for k in range(2):
        row = k * (R - 1)

        @pl.when(reach[k])
        def _():
            part_copy(1 - k).wait_recv()
            acc2[row] += pr[k].astype(f32)

        finish(row)

    for cv, ds in ((ONE, range(8)), (COARSE, range(8)), (TWO, col_ds)):
        sides("send", cv, ds)
        cross("send", cv, col_ds)
    when_second(*[cp.wait_send for cp in to_first])
    when_first(*[cp.wait_send for cp in to_second])
    for k in range(2):
        @pl.when(reach[k])
        def _():
            part_copy(k).wait_send()


def store(src, dst, sem):
    cp = pltpu.make_async_copy(src, dst, sem)
    cp.start()
    cp.wait()


def per_device(latent, proj_weight, proj_bias, cache_one, cache_two,
               conv_one, bias_one, conv_two, bias_two):
    _, R, W, CH = cache_one.shape
    _, HR, HW, LCH = latent.shape
    WP, HP = W + 2 * EDGE, HW + 2 * EDGE
    anywhere = pl.BlockSpec(memory_space=pl.ANY)
    bf, f32 = jnp.bfloat16, jnp.float32
    dma = pltpu.SemaphoreType.DMA
    decoded = pl.pallas_call(
        functools.partial(kernel, lax.axis_size("row"), lax.axis_size("col")),
        out_shape=pltpu.VMEM(cache_one.shape, bf),
        in_specs=[anywhere] * 9,
        out_specs=pl.BlockSpec(memory_space=pltpu.VMEM),
        scratch_shapes=[
            pltpu.VMEM((HR, HW, LCH), bf),
            pltpu.VMEM((LCH, CH), bf),
            pltpu.VMEM((2, 3, 3, CH, 3 * CH), bf),
            pltpu.VMEM((2, 4 * CH, 4 * CH), bf),
            pltpu.VMEM((2, R + 2, WP, CH), bf),
            pltpu.VMEM((HR + 2, HP, CH), bf),
            pltpu.VMEM((HR + 2, HP, CH), bf),
            pltpu.VMEM((3, R + 2, WP, CH), bf),
            pltpu.VMEM((HR, W, CH), bf),
            pltpu.VMEM((R * WP, CH), f32),
            pltpu.VMEM((R, W, CH), f32),
            pltpu.VMEM((W, CH), f32),
            pltpu.VMEM((2, W, CH), bf),
            pltpu.VMEM((2, W, CH), bf),
            pltpu.VMEM((1, CH), f32),
            pltpu.VMEM((1, CH), f32),
            pltpu.VMEM((1, CH), f32),
            dma((13,)), dma((3, 8)), dma((3, 8)), dma((3, 2)), dma((3, 2)),
            dma((2, 3)), dma((2, 3)), dma((2,)), dma((2,)),
        ],
        compiler_params=pltpu.CompilerParams(
            collective_id=0, has_side_effects=True, vmem_limit_bytes=60 * 1024 * 1024),
        name="decoder_window",
    )(latent, proj_weight, proj_bias.reshape(1, CH), cache_one, cache_two,
      conv_one, bias_one.reshape(1, CH), conv_two, bias_two.reshape(1, CH))
    return pl.pallas_call(
        store,
        out_shape=jax.ShapeDtypeStruct(cache_one.shape, bf),
        in_specs=[pl.BlockSpec(memory_space=pltpu.VMEM)],
        out_specs=anywhere,
        scratch_shapes=[dma],
        compiler_params=pltpu.CompilerParams(vmem_limit_bytes=1024 * 1024),
        name="store",
    )(decoded)


def solution(mesh):
    placed = P(("grp", "frm"), "row", "col", None)
    return jax.shard_map(
        per_device,
        mesh=mesh,
        in_specs=(placed, P(), P(), placed, placed, P(), P(), P(), P()),
        out_specs=placed,
        check_vma=False,
    )
```

```python
import functools

import jax
import jax.numpy as jnp
from jax import lax
from jax.experimental import pallas as pl
from jax.experimental.pallas import tpu as pltpu
from jax.sharding import PartitionSpec as P

EDGE = 16
MESH = pl.DeviceIdType.MESH
SIDES = [(-1, 0), (1, 0), (0, -1), (0, 1), (-1, -1), (-1, 1), (1, -1), (1, 1)]
ONE, COARSE, TWO = 0, 1, 2
MIDDLE = (1, 0, 1)


def kernel(rows_n, cols_n, lat_h, pw_h, pb_h, c1_h, c2_h, w1_h, b1_h, w2_h, b2_h, out_v,
           lat, pw, w, wu, F1, CA, CB, F2, up, acc1, acc2, s1, ps, pr, pb, b1, b2,
           load_sem, side_send, side_recv, cross_send, cross_recv,
           mid_send, mid_recv, part_send, part_recv):
    R, W, CH = c1_h.shape[1], c1_h.shape[2], c1_h.shape[3]
    HR, HW = lat.shape[0], lat.shape[1]
    WP, HP = W + 2 * EDGE, HW + 2 * EDGE
    bf, f32 = jnp.bfloat16, jnp.float32
    r, c, f = lax.axis_index("row"), lax.axis_index("col"), lax.axis_index("frm")
    up_ok, down_ok = r > 0, r < rows_n - 1
    left_ok, right_ok = c > 0, c < cols_n - 1
    first, second = f == 0, f == 1

    def exists(d):
        dr, dc = SIDES[d]
        ok = None
        for test in ([up_ok] if dr < 0 else [down_ok] if dr > 0 else []) + (
                [left_ok] if dc < 0 else [right_ok] if dc > 0 else []):
            ok = test if ok is None else jnp.logical_and(ok, test)
        return ok

    def where_is(d):
        dr, dc = SIDES[d]
        ids = {}
        if dr:
            ids["row"] = r + dr
        if dc:
            ids["col"] = c + dc
        return ids

    def opposite(d):
        return SIDES.index((-SIDES[d][0], -SIDES[d][1]))

    loads = []

    def load(src, dst):
        cp = pltpu.make_async_copy(src, dst, load_sem.at[len(loads)])
        cp.start()
        loads.append(cp)
        return cp

    def load_weights(cv, src):
        return [load(src.at[:, :, q], w.at[cv, :, :, :, pl.ds(q * CH, CH)]) for q in range(3)]

    first_cp = [load(lat_h.at[0], lat), load(pw_h, pw), load(pb_h, pb)]
    two_cp = [load(c2_h.at[0], F2.at[0, pl.ds(1, R), pl.ds(0, W)])] + load_weights(1, w2_h)
    w_cp = load_weights(0, w1_h)
    one_cp = [load(c1_h.at[0], F1.at[0, pl.ds(1, R), pl.ds(0, W)]), load(b1_h, b1), load(b2_h, b2)]

    partner = {"frm": 1 - f}
    barrier = pltpu.get_barrier_semaphore()
    for d in range(8):
        @pl.when(exists(d))
        def _():
            for ids in ({}, partner)[:2 if SIDES[d][0] == 0 else 1]:
                pl.semaphore_signal(barrier, inc=1, device_id={**where_is(d), **ids},
                                    device_id_type=MESH)
    pl.semaphore_signal(barrier, inc=1, device_id=partner, device_id_type=MESH)

    def clear(ref, *place):
        shape = ref.at[place].shape
        ref[place] = jnp.zeros(shape, bf)

    rims = ((left_ok, lambda n: pl.ds(n - EDGE, EDGE)), (right_ok, lambda n: pl.ds(n - 2 * EDGE, EDGE)))
    for ref, tall, wide in ((F1.at[0], R, WP), (CA, HR, HP)):
        for ok, row in ((up_ok, 0), (down_ok, tall + 1)):
            @pl.when(jnp.logical_not(ok))
            def _():
                clear(ref, row, pl.ds(0, wide))
        for ok, rim in rims:
            @pl.when(jnp.logical_not(ok))
            def _():
                clear(ref, pl.ds(0, tall + 2), rim(wide))
    for ok, rim in rims:
        @pl.when(jnp.logical_not(ok))
        def _():
            clear(F2, 0, pl.ds(1, R), rim(WP))

            @pl.when(first)
            def _():
                clear(F1, 1, pl.ds(1, R), rim(WP))
                clear(F2, 1, pl.ds(1, R), rim(WP))

            @pl.when(second)
            def _():
                clear(CB, pl.ds(1, HR), rim(HP))
    for a in range(3):
        for row in (0, R + 1):
            clear(F2, a, row, pl.ds(0, WP))

    for cp in first_cp:
        cp.wait()

    def project(i, carry):
        v = jnp.dot(lat[i], pw[...], preferred_element_type=f32) + pb[...]
        v = v.astype(bf).astype(f32)
        CA[1 + i, pl.ds(0, HW)] = (v / (1.0 + jnp.exp(-v))).astype(bf)
        for k in range(2):
            s1[pl.ds(k, HW, stride=2), :] = v
        up[i] = s1[...].astype(bf)
        return carry

    lax.fori_loop(0, HR, project, 0)

    def side_refs(cv, d, slot=0):
        dr, dc = SIDES[d]
        n, m = (HR, HW) if cv == COARSE else (R, W)
        row, land_row = (0, n + 1) if dr < 0 else (n - 1, 0)
        col, land_col = ((0, m) if dc < 0 else (m - EDGE, m + EDGE))
        rows, land_rows = (pl.ds(row, 1), pl.ds(land_row, 1)) if dr else (pl.ds(0, n), pl.ds(1, n))
        cols, land_cols = (
            (pl.ds(col, EDGE), pl.ds(land_col, EDGE)) if dc else (pl.ds(0, m), pl.ds(0, m)))
        if cv == COARSE:
            src = CA.at[pl.ds(1 + rows.start, rows.size), cols]
            return src, (CB if slot else CA).at[land_rows, land_cols]
        src = (c1_h, c2_h)[cv // 2].at[0, rows, cols]
        return src, (F1, F2)[cv // 2].at[slot, land_rows, land_cols]

    def side_copy(cv, d):
        src, dst = side_refs(cv, d)
        return pltpu.make_async_remote_copy(
            src_ref=src, dst_ref=dst, send_sem=side_send.at[cv, d], recv_sem=side_recv.at[cv, d],
            device_id=where_is(d), device_id_type=MESH)

    def cross_copy(cv, d):
        src, dst = side_refs(cv, d, 1)
        return pltpu.make_async_remote_copy(
            src_ref=src, dst_ref=dst, send_sem=cross_send.at[cv, d - 2],
            recv_sem=cross_recv.at[cv, d - 2], device_id={**where_is(d), **partner},
            device_id_type=MESH)

    tall_ds, col_ds = (0, 1, 4, 5, 6, 7), (2, 3)

    def sides(act, cv, ds):
        for d in ds:
            @pl.when(exists(opposite(d) if act == "recv" else d))
            def _():
                cp = side_copy(cv, d)
                {"start": cp.start, "recv": cp.wait_recv, "send": cp.wait_send}[act]()

    def cross(act, cv, ds):
        owner = f == MIDDLE[cv]
        for d in ds:
            there = exists(opposite(d) if act == "recv" else d)

            @pl.when(jnp.logical_and(there, jnp.logical_not(owner) if act == "recv" else owner))
            def _():
                cp = cross_copy(cv, d)
                {"start": cp.start, "recv": cp.wait_recv, "send": cp.wait_send}[act]()

    def to_partner(cv, k, src, dst):
        return pltpu.make_async_remote_copy(
            src_ref=src, dst_ref=dst, send_sem=mid_send.at[cv, k], recv_sem=mid_recv.at[cv, k],
            device_id=partner, device_id_type=MESH)

    all_w, all_h = pl.ds(0, WP), pl.ds(0, HP)
    to_first = [
        to_partner(0, 0, c1_h.at[0], F1.at[1, pl.ds(1, R), pl.ds(0, W)]),
        to_partner(0, 1, F1.at[0, 0, all_w], F1.at[1, 0, all_w]),
        to_partner(0, 2, F1.at[0, R + 1, all_w], F1.at[1, R + 1, all_w]),
        to_partner(1, 0, c2_h.at[0], F2.at[1, pl.ds(1, R), pl.ds(0, W)])]
    main = pl.ds(1, HR), pl.ds(0, HW)
    to_second = [
        to_partner(0, 0, CA.at[main], CB.at[main]),
        to_partner(1, 0, F2.at[2, 1, all_w], F2.at[1, 1, all_w]),
        to_partner(1, 1, F2.at[2, R, all_w], F2.at[1, R, all_w]),
        to_partner(1, 2, F2.at[2, pl.ds(2, R - 2), all_w], F2.at[1, pl.ds(2, R - 2), all_w]),
        to_partner(0, 1, CA.at[0, all_h], CB.at[0, all_h]),
        to_partner(0, 2, CA.at[HR + 1, all_h], CB.at[HR + 1, all_h])]

    def when_first(*bodies):
        @pl.when(first)
        def _():
            for body in bodies:
                body()

    def when_second(*bodies):
        @pl.when(second)
        def _():
            for body in bodies:
                body()

    def weights(cv, frames):
        return jnp.concatenate([w[cv, a].reshape(3 * CH, 3 * CH) for a in frames], axis=0)

    def fold_taps(place, a):
        k0, k1, k2 = (w[0, a, p].astype(f32) for p in range(3))
        for parity, pair in ((0, (k0, k1 + k2)), (1, (k0 + k1, k2))):
            for b, m in enumerate(pair):
                q0, q1, q2 = m[:, :CH], m[:, CH:2 * CH], m[:, 2 * CH:]
                wu[parity, pl.ds((2 * place + b) * CH, CH)] = jnp.concatenate(
                    [q1 + q2, q0 + q1, q0, q2], axis=1).astype(bf)

    spot = lax.broadcasted_iota(jnp.int32, (8, CH), 0)

    def fold_main(z):
        after = pltpu.roll(z[:, :CH], 1, 0)
        after = jnp.concatenate([jnp.where(spot == 0, 0.0, after[:8]), after[8:]], axis=0)
        ahead = pltpu.roll(z[:, 2 * CH:], W - 1, 0)
        ahead = jnp.concatenate([ahead[:W - 8], jnp.where(spot == 7, 0.0, ahead[W - 8:])], axis=0)
        return after + z[:, CH:2 * CH] + ahead

    def fold_ring(z):
        n = z.shape[0]
        return pltpu.roll(z[:, :CH], 1, 0) + z[:, CH:2 * CH] + pltpu.roll(z[:, 2 * CH:], n - 1, 0)

    def second_main(frames, at=0, size=R):
        lhs = jnp.concatenate(
            [F2[a, pl.ds(at + p, size), pl.ds(0, W)].reshape(size * W, CH)
             for a in frames for p in range(3)], axis=1)
        z = jnp.dot(lhs, weights(1, frames), preferred_element_type=f32)
        return [fold_main(z[n * W:(n + 1) * W]) for n in range(size)]

    def own_two(at, size):
        for n, y in enumerate(second_main((0,), at, size)):
            acc2[at + n] = y

    tall = 1 + up_ok.astype(jnp.int32) + down_ok.astype(jnp.int32)
    wide = 1 + left_ok.astype(jnp.int32) + right_ok.astype(jnp.int32)
    pl.semaphore_wait(barrier, tall * wide + wide - 1)
    sides("start", ONE, (4, 5, 6, 7))
    sides("start", COARSE, (4, 5, 6, 7))
    when_second(lambda: sides("start", ONE, (0, 1)))
    sides("start", ONE, col_ds)
    cross("start", ONE, col_ds)
    when_second(to_first[0].start)
    when_first(to_second[0].start)
    sides("start", COARSE, (0, 1, 2, 3))
    cross("start", COARSE, col_ds)
    when_first(lambda: sides("start", ONE, (0, 1)))

    for cp in two_cp:
        cp.wait()
    own_two(0, R)
    when_second(to_first[3].start)
    sides("start", TWO, col_ds)
    cross("start", TWO, col_ds)

    for cp in w_cp:
        cp.wait()
    fold_taps(0, 2)
    when_second(lambda: fold_taps(1, 1))

    def inside_dot(frames, at, n):
        lhs = jnp.concatenate(
            [F1[a, pl.ds(1 + p, R - 2), pl.ds(at, n)].reshape((R - 2) * n, CH)
             for a in frames for p in range(3)], axis=1)
        z = jnp.dot(lhs, weights(0, frames), preferred_element_type=f32)
        return [z[k * n:(k + 1) * n] for k in range(R - 2)]

    def inside_main(frames):
        for k, z in enumerate(inside_dot(frames, 0, W)):
            z = jnp.concatenate([z, jnp.zeros((2 * EDGE, 3 * CH), f32)], axis=0)
            acc1[pl.ds((1 + k) * WP, WP)] = fold_ring(z)

    def inside_rim(frames):
        rest = jnp.zeros((EDGE, 3 * CH), f32)
        for k, z in enumerate(inside_dot(frames, W, 2 * EDGE)):
            y = fold_ring(jnp.concatenate([rest, z, rest], axis=0))
            acc1[pl.ds((1 + k) * WP + W - EDGE, 3 * EDGE)] += y[:3 * EDGE]
            acc1[pl.ds((1 + k) * WP, EDGE)] += y[3 * EDGE:]

    def border_line(k):
        return pl.ds(k * (R - 1) * WP, WP)

    def border_dot(frames, rows, taps):
        lhs = jnp.concatenate([F1[a, row] for a in frames for row in rows], axis=1)
        rhs = jnp.concatenate([w[0, a, p] for a in frames for p in taps], axis=0)
        return fold_ring(jnp.dot(lhs, rhs, preferred_element_type=f32))

    def border_own(frames):
        for k in range(2):
            acc1[border_line(k)] = border_dot(frames, ((1, 2), (R - 1, R))[k], ((1, 2), (0, 1))[k])

    def border_halo(frames, k):
        acc1[border_line(k)] += border_dot(frames, (k * (R + 1),), (2 * k,))

    def coarse(frames):
        for parity in range(2):
            lhs = jnp.concatenate(
                [ref[pl.ds(parity + b, HR)].reshape(HR * HP, CH) for ref in frames for b in range(2)],
                axis=1)
            z = jnp.dot(lhs, wu[parity, pl.ds(0, 2 * CH * len(frames))], preferred_element_type=f32)
            for i in range(HR):
                zi = z[i * HP:(i + 1) * HP]
                even = zi[:, :CH] + pltpu.roll(zi[:, 2 * CH:3 * CH], 1, 0)
                odd = zi[:, CH:2 * CH] + pltpu.roll(zi[:, 3 * CH:], HP - 1, 0)
                base = (2 * i + parity) * WP
                for at, n, to in ((0, HW, 0), (HW, EDGE // 2, W), (HP - EDGE // 2, EDGE // 2, WP - EDGE)):
                    for k, y in ((0, even), (1, odd)):
                        acc1[pl.ds(base + to + k, n, stride=2), :] += y[at:at + n]

    def act_two(row):
        y = acc1[pl.ds(row * WP, WP)] + b1[...]
        y = y / (1.0 + jnp.exp(-y))
        F2[2, 1 + row, pl.ds(0, W)] = y[:W].astype(bf)
        F2[2, 1 + row, pl.ds(W, EDGE)] = jnp.where(right_ok, y[W:W + EDGE], 0.0).astype(bf)
        F2[2, 1 + row, pl.ds(W + EDGE, EDGE)] = jnp.where(left_ok, y[W + EDGE:], 0.0).astype(bf)

    def inner(k, carry):
        act_two(1 + k)
        return carry

    def act_inside():
        lax.fori_loop(0, R - 2, inner, 0)

    for cp in one_cp:
        cp.wait()

    @pl.when(second)
    def _():
        inside_main((0,))
        sides("recv", ONE, tall_ds)
        to_first[1].start()
        to_first[2].start()
        sides("recv", ONE, col_ds)
        inside_rim((0,))
        border_own((0,))
        for k in range(2):
            border_halo((0,), k)
        sides("recv", COARSE, range(8))
        cross("recv", COARSE, col_ds)
        for i in (0, 4, 5):
            to_second[i].wait_recv()
        coarse((CA, CB))

    @pl.when(first)
    def _():
        to_first[0].wait_recv()
        inside_main((0, 1))
        sides("recv", ONE, col_ds)
        cross("recv", ONE, col_ds)
        inside_rim((0, 1))
        border_own((0, 1))
        sides("recv", COARSE, range(8))
        to_second[4].start()
        to_second[5].start()
        coarse((CA,))
        act_inside()
        to_second[3].start()
        sides("recv", ONE, tall_ds)
        to_first[1].wait_recv()
        to_first[2].wait_recv()

    def part_copy(k):
        return pltpu.make_async_remote_copy(
            src_ref=ps.at[k], dst_ref=pr.at[1 - k], send_sem=part_send.at[k],
            recv_sem=part_recv.at[1 - k], device_id={"row": r - 1 + 2 * k}, device_id_type=MESH)

    reach = (up_ok, down_ok)

    def send_part(k):
        lhs = jnp.concatenate([F2[a, 1 + k * (R - 1)] for a in range(3)], axis=1)
        rhs = jnp.concatenate([w[1, a, 2 - 2 * k] for a in range(3)], axis=0)
        ps[k] = fold_ring(jnp.dot(lhs, rhs, preferred_element_type=f32))[:W].astype(bf)

        @pl.when(reach[k])
        def _():
            part_copy(k).start()

    @pl.when(first)
    def _():
        sides("recv", TWO, col_ds)
        cross("recv", TWO, col_ds)
        to_first[3].wait_recv()
        for k in range(2):
            border_halo((0, 1), k)
            act_two(k * (R - 1))
            to_second[1 + k].start()
            send_part(k)

    @pl.when(second)
    def _():
        for k in range(2):
            act_two(k * (R - 1))
        act_inside()
        sides("recv", TWO, col_ds)
        for k in range(2):
            to_second[1 + k].wait_recv()
            send_part(k)

    when_second(to_second[3].wait_recv)
    for n, y in enumerate(second_main((1, 2))):
        acc2[n] += y

    lhs = jnp.concatenate(
        [F2[a, pl.ds(p, R), pl.ds(W, 2 * EDGE)].reshape(R * 2 * EDGE, CH)
         for a in range(3) for p in range(3)], axis=1)
    z = jnp.dot(lhs, weights(1, range(3)), preferred_element_type=f32)
    for n in range(R):
        part = z[n * 2 * EDGE:(n + 1) * 2 * EDGE]
        acc2[n, pl.ds(0, 1)] += part[2 * EDGE - 1:, :CH]
        acc2[n, pl.ds(W - 1, 1)] += part[:1, 2 * CH:]

    def finish(row):
        y = acc2[row] + b2[...] + up[row // 2].astype(f32)
        out_v[0, row] = y.astype(bf)

    def last(k, carry):
        finish(1 + k)
        return carry

    lax.fori_loop(0, R - 2, last, 0)
    for k in range(2):
        row = k * (R - 1)

        @pl.when(reach[k])
        def _():
            part_copy(1 - k).wait_recv()
            acc2[row] += pr[k].astype(f32)

        finish(row)

    for cv, ds in ((ONE, range(8)), (COARSE, range(8)), (TWO, col_ds)):
        sides("send", cv, ds)
        cross("send", cv, col_ds)
    when_second(*[cp.wait_send for cp in to_first])
    when_first(*[cp.wait_send for cp in to_second])
    for k in range(2):
        @pl.when(reach[k])
        def _():
            part_copy(k).wait_send()


def store(src, dst, sem):
    cp = pltpu.make_async_copy(src, dst, sem)
    cp.start()
    cp.wait()


def per_device(latent, proj_weight, proj_bias, cache_one, cache_two,
               conv_one, bias_one, conv_two, bias_two):
    _, R, W, CH = cache_one.shape
    _, HR, HW, LCH = latent.shape
    WP, HP = W + 2 * EDGE, HW + 2 * EDGE
    anywhere = pl.BlockSpec(memory_space=pl.ANY)
    bf, f32 = jnp.bfloat16, jnp.float32
    dma = pltpu.SemaphoreType.DMA
    decoded = pl.pallas_call(
        functools.partial(kernel, lax.axis_size("row"), lax.axis_size("col")),
        out_shape=pltpu.VMEM(cache_one.shape, bf),
        in_specs=[anywhere] * 9,
        out_specs=pl.BlockSpec(memory_space=pltpu.VMEM),
        scratch_shapes=[
            pltpu.VMEM((HR, HW, LCH), bf),
            pltpu.VMEM((LCH, CH), bf),
            pltpu.VMEM((2, 3, 3, CH, 3 * CH), bf),
            pltpu.VMEM((2, 4 * CH, 4 * CH), bf),
            pltpu.VMEM((2, R + 2, WP, CH), bf),
            pltpu.VMEM((HR + 2, HP, CH), bf),
            pltpu.VMEM((HR + 2, HP, CH), bf),
            pltpu.VMEM((3, R + 2, WP, CH), bf),
            pltpu.VMEM((HR, W, CH), bf),
            pltpu.VMEM((R * WP, CH), f32),
            pltpu.VMEM((R, W, CH), f32),
            pltpu.VMEM((W, CH), f32),
            pltpu.VMEM((2, W, CH), bf),
            pltpu.VMEM((2, W, CH), bf),
            pltpu.VMEM((1, CH), f32),
            pltpu.VMEM((1, CH), f32),
            pltpu.VMEM((1, CH), f32),
            dma((13,)), dma((3, 8)), dma((3, 8)), dma((3, 2)), dma((3, 2)),
            dma((2, 3)), dma((2, 3)), dma((2,)), dma((2,)),
        ],
        compiler_params=pltpu.CompilerParams(
            collective_id=0, has_side_effects=True, vmem_limit_bytes=60 * 1024 * 1024),
        name="decoder_window",
    )(latent, proj_weight, proj_bias.reshape(1, CH), cache_one, cache_two,
      conv_one, bias_one.reshape(1, CH), conv_two, bias_two.reshape(1, CH))
    return pl.pallas_call(
        store,
        out_shape=jax.ShapeDtypeStruct(cache_one.shape, bf),
        in_specs=[pl.BlockSpec(memory_space=pltpu.VMEM)],
        out_specs=anywhere,
        scratch_shapes=[dma],
        compiler_params=pltpu.CompilerParams(vmem_limit_bytes=1024 * 1024),
        name="store",
    )(decoded)


def solution(mesh):
    placed = P(("grp", "frm"), "row", "col", None)
    return jax.shard_map(
        per_device,
        mesh=mesh,
        in_specs=(placed, P(), P(), placed, placed, P(), P(), P(), P()),
        out_specs=placed,
        check_vma=False,
    )
```

```python
import functools

import jax
import jax.numpy as jnp
from jax import lax
from jax.experimental import pallas as pl
from jax.experimental.pallas import tpu as pltpu
from jax.sharding import PartitionSpec as P

EDGE = 16
MESH = pl.DeviceIdType.MESH
SIDES = [(-1, 0), (1, 0), (0, -1), (0, 1), (-1, -1), (-1, 1), (1, -1), (1, 1)]
ONE, COARSE, TWO = 0, 1, 2
MIDDLE = (1, 0, 1)


def kernel(rows_n, cols_n, lat_h, pw_h, pb_h, c1_h, c2_h, w1_h, b1_h, w2_h, b2_h, out_v,
           lat, pw, w, wu, F1, CA, CB, F2, up, acc1, acc2, s1, ps, pr, pb, b1, b2,
           load_sem, side_send, side_recv, cross_send, cross_recv,
           mid_send, mid_recv, part_send, part_recv):
    R, W, CH = c1_h.shape[1], c1_h.shape[2], c1_h.shape[3]
    HR, HW = lat.shape[0], lat.shape[1]
    WP, HP = W + 2 * EDGE, HW + 2 * EDGE
    bf, f32 = jnp.bfloat16, jnp.float32
    r, c, f = lax.axis_index("row"), lax.axis_index("col"), lax.axis_index("frm")
    up_ok, down_ok = r > 0, r < rows_n - 1
    left_ok, right_ok = c > 0, c < cols_n - 1
    first, second = f == 0, f == 1

    def exists(d):
        dr, dc = SIDES[d]
        ok = None
        for test in ([up_ok] if dr < 0 else [down_ok] if dr > 0 else []) + (
                [left_ok] if dc < 0 else [right_ok] if dc > 0 else []):
            ok = test if ok is None else jnp.logical_and(ok, test)
        return ok

    def where_is(d):
        dr, dc = SIDES[d]
        ids = {}
        if dr:
            ids["row"] = r + dr
        if dc:
            ids["col"] = c + dc
        return ids

    def opposite(d):
        return SIDES.index((-SIDES[d][0], -SIDES[d][1]))

    loads = []

    def load(src, dst):
        cp = pltpu.make_async_copy(src, dst, load_sem.at[len(loads)])
        cp.start()
        loads.append(cp)
        return cp

    def load_weights(cv, src):
        return [load(src.at[:, :, q], w.at[cv, :, :, :, pl.ds(q * CH, CH)]) for q in range(3)]

    first_cp = [load(lat_h.at[0], lat), load(pw_h, pw), load(pb_h, pb)]
    two_cp = [load(c2_h.at[0], F2.at[0, pl.ds(1, R), pl.ds(0, W)])] + load_weights(1, w2_h)
    w_cp = load_weights(0, w1_h)
    one_cp = [load(c1_h.at[0], F1.at[0, pl.ds(1, R), pl.ds(0, W)]), load(b1_h, b1), load(b2_h, b2)]

    partner = {"frm": 1 - f}
    barrier = pltpu.get_barrier_semaphore()
    for d in range(8):
        @pl.when(exists(d))
        def _():
            for ids in ({}, partner)[:2 if SIDES[d][0] == 0 else 1]:
                pl.semaphore_signal(barrier, inc=1, device_id={**where_is(d), **ids},
                                    device_id_type=MESH)
    pl.semaphore_signal(barrier, inc=1, device_id=partner, device_id_type=MESH)

    def clear(ref, *place):
        shape = ref.at[place].shape
        ref[place] = jnp.zeros(shape, bf)

    rims = ((left_ok, lambda n: pl.ds(n - EDGE, EDGE)), (right_ok, lambda n: pl.ds(n - 2 * EDGE, EDGE)))
    for ref, tall, wide in ((F1.at[0], R, WP), (CA, HR, HP)):
        for ok, row in ((up_ok, 0), (down_ok, tall + 1)):
            @pl.when(jnp.logical_not(ok))
            def _():
                clear(ref, row, pl.ds(0, wide))
        for ok, rim in rims:
            @pl.when(jnp.logical_not(ok))
            def _():
                clear(ref, pl.ds(0, tall + 2), rim(wide))
    for ok, rim in rims:
        @pl.when(jnp.logical_not(ok))
        def _():
            clear(F2, 0, pl.ds(1, R), rim(WP))

            @pl.when(first)
            def _():
                clear(F1, 1, pl.ds(1, R), rim(WP))
                clear(F2, 1, pl.ds(1, R), rim(WP))

            @pl.when(second)
            def _():
                clear(CB, pl.ds(1, HR), rim(HP))
    for a in range(3):
        for row in (0, R + 1):
            clear(F2, a, row, pl.ds(0, WP))

    for cp in first_cp:
        cp.wait()

    def project(i, carry):
        v = jnp.dot(lat[i], pw[...], preferred_element_type=f32) + pb[...]
        v = v.astype(bf).astype(f32)
        CA[1 + i, pl.ds(0, HW)] = (v / (1.0 + jnp.exp(-v))).astype(bf)
        for k in range(2):
            s1[pl.ds(k, HW, stride=2), :] = v
        up[i] = s1[...].astype(bf)
        return carry

    lax.fori_loop(0, HR, project, 0)

    def side_refs(cv, d, slot=0):
        dr, dc = SIDES[d]
        n, m = (HR, HW) if cv == COARSE else (R, W)
        row, land_row = (0, n + 1) if dr < 0 else (n - 1, 0)
        col, land_col = ((0, m) if dc < 0 else (m - EDGE, m + EDGE))
        rows, land_rows = (pl.ds(row, 1), pl.ds(land_row, 1)) if dr else (pl.ds(0, n), pl.ds(1, n))
        cols, land_cols = (
            (pl.ds(col, EDGE), pl.ds(land_col, EDGE)) if dc else (pl.ds(0, m), pl.ds(0, m)))
        if cv == COARSE:
            src = CA.at[pl.ds(1 + rows.start, rows.size), cols]
            return src, (CB if slot else CA).at[land_rows, land_cols]
        src = (c1_h, c2_h)[cv // 2].at[0, rows, cols]
        return src, (F1, F2)[cv // 2].at[slot, land_rows, land_cols]

    def side_copy(cv, d):
        src, dst = side_refs(cv, d)
        return pltpu.make_async_remote_copy(
            src_ref=src, dst_ref=dst, send_sem=side_send.at[cv, d], recv_sem=side_recv.at[cv, d],
            device_id=where_is(d), device_id_type=MESH)

    def cross_copy(cv, d):
        src, dst = side_refs(cv, d, 1)
        return pltpu.make_async_remote_copy(
            src_ref=src, dst_ref=dst, send_sem=cross_send.at[cv, d - 2],
            recv_sem=cross_recv.at[cv, d - 2], device_id={**where_is(d), **partner},
            device_id_type=MESH)

    tall_ds, col_ds = (0, 1, 4, 5, 6, 7), (2, 3)

    def sides(act, cv, ds):
        for d in ds:
            @pl.when(exists(opposite(d) if act == "recv" else d))
            def _():
                cp = side_copy(cv, d)
                {"start": cp.start, "recv": cp.wait_recv, "send": cp.wait_send}[act]()

    def cross(act, cv, ds):
        owner = f == MIDDLE[cv]
        for d in ds:
            there = exists(opposite(d) if act == "recv" else d)

            @pl.when(jnp.logical_and(there, jnp.logical_not(owner) if act == "recv" else owner))
            def _():
                cp = cross_copy(cv, d)
                {"start": cp.start, "recv": cp.wait_recv, "send": cp.wait_send}[act]()

    def to_partner(cv, k, src, dst):
        return pltpu.make_async_remote_copy(
            src_ref=src, dst_ref=dst, send_sem=mid_send.at[cv, k], recv_sem=mid_recv.at[cv, k],
            device_id=partner, device_id_type=MESH)

    all_w, all_h = pl.ds(0, WP), pl.ds(0, HP)
    to_first = [
        to_partner(0, 0, c1_h.at[0], F1.at[1, pl.ds(1, R), pl.ds(0, W)]),
        to_partner(0, 1, F1.at[0, 0, all_w], F1.at[1, 0, all_w]),
        to_partner(0, 2, F1.at[0, R + 1, all_w], F1.at[1, R + 1, all_w]),
        to_partner(1, 0, c2_h.at[0], F2.at[1, pl.ds(1, R), pl.ds(0, W)])]
    main = pl.ds(1, HR), pl.ds(0, HW)
    to_second = [
        to_partner(0, 0, CA.at[main], CB.at[main]),
        to_partner(1, 0, F2.at[2, 1, all_w], F2.at[1, 1, all_w]),
        to_partner(1, 1, F2.at[2, R, all_w], F2.at[1, R, all_w]),
        to_partner(1, 2, F2.at[2, pl.ds(2, R - 2), all_w], F2.at[1, pl.ds(2, R - 2), all_w]),
        to_partner(0, 1, CA.at[0, all_h], CB.at[0, all_h]),
        to_partner(0, 2, CA.at[HR + 1, all_h], CB.at[HR + 1, all_h])]

    def when_first(*bodies):
        @pl.when(first)
        def _():
            for body in bodies:
                body()

    def when_second(*bodies):
        @pl.when(second)
        def _():
            for body in bodies:
                body()

    def weights(cv, frames):
        return jnp.concatenate([w[cv, a].reshape(3 * CH, 3 * CH) for a in frames], axis=0)

    def fold_taps(place, a):
        k0, k1, k2 = (w[0, a, p].astype(f32) for p in range(3))
        for parity, pair in ((0, (k0, k1 + k2)), (1, (k0 + k1, k2))):
            for b, m in enumerate(pair):
                q0, q1, q2 = m[:, :CH], m[:, CH:2 * CH], m[:, 2 * CH:]
                wu[parity, pl.ds((2 * place + b) * CH, CH)] = jnp.concatenate(
                    [q1 + q2, q0 + q1, q0, q2], axis=1).astype(bf)

    spot = lax.broadcasted_iota(jnp.int32, (8, CH), 0)

    def fold_main(z):
        after = pltpu.roll(z[:, :CH], 1, 0)
        after = jnp.concatenate([jnp.where(spot == 0, 0.0, after[:8]), after[8:]], axis=0)
        ahead = pltpu.roll(z[:, 2 * CH:], W - 1, 0)
        ahead = jnp.concatenate([ahead[:W - 8], jnp.where(spot == 7, 0.0, ahead[W - 8:])], axis=0)
        return after + z[:, CH:2 * CH] + ahead

    def fold_ring(z):
        n = z.shape[0]
        return pltpu.roll(z[:, :CH], 1, 0) + z[:, CH:2 * CH] + pltpu.roll(z[:, 2 * CH:], n - 1, 0)

    def second_main(frames, at=0, size=R):
        lhs = jnp.concatenate(
            [F2[a, pl.ds(at + p, size), pl.ds(0, W)].reshape(size * W, CH)
             for a in frames for p in range(3)], axis=1)
        z = jnp.dot(lhs, weights(1, frames), preferred_element_type=f32)
        return [fold_main(z[n * W:(n + 1) * W]) for n in range(size)]

    def own_two(at, size):
        for n, y in enumerate(second_main((0,), at, size)):
            acc2[at + n] = y

    tall = 1 + up_ok.astype(jnp.int32) + down_ok.astype(jnp.int32)
    wide = 1 + left_ok.astype(jnp.int32) + right_ok.astype(jnp.int32)
    pl.semaphore_wait(barrier, tall * wide + wide - 1)
    sides("start", ONE, (4, 5, 6, 7))
    sides("start", COARSE, (4, 5, 6, 7))
    when_second(lambda: sides("start", ONE, (0, 1)))
    sides("start", ONE, col_ds)
    cross("start", ONE, col_ds)
    when_second(to_first[0].start)
    when_first(to_second[0].start)
    sides("start", COARSE, (0, 1, 2, 3))
    cross("start", COARSE, col_ds)
    when_first(lambda: sides("start", ONE, (0, 1)))

    for cp in two_cp:
        cp.wait()
    own_two(0, R)
    when_second(to_first[3].start)
    sides("start", TWO, col_ds)
    cross("start", TWO, col_ds)

    for cp in w_cp:
        cp.wait()
    fold_taps(0, 2)
    when_second(lambda: fold_taps(1, 1))

    def inside_dot(frames, at, n):
        lhs = jnp.concatenate(
            [F1[a, pl.ds(1 + p, R - 2), pl.ds(at, n)].reshape((R - 2) * n, CH)
             for a in frames for p in range(3)], axis=1)
        z = jnp.dot(lhs, weights(0, frames), preferred_element_type=f32)
        return [z[k * n:(k + 1) * n] for k in range(R - 2)]

    def inside_main(frames):
        for k, z in enumerate(inside_dot(frames, 0, W)):
            z = jnp.concatenate([z, jnp.zeros((2 * EDGE, 3 * CH), f32)], axis=0)
            acc1[pl.ds((1 + k) * WP, WP)] = fold_ring(z)

    def inside_rim(frames):
        rest = jnp.zeros((EDGE, 3 * CH), f32)
        for k, z in enumerate(inside_dot(frames, W, 2 * EDGE)):
            y = fold_ring(jnp.concatenate([rest, z, rest], axis=0))
            acc1[pl.ds((1 + k) * WP + W - EDGE, 3 * EDGE)] += y[:3 * EDGE]
            acc1[pl.ds((1 + k) * WP, EDGE)] += y[3 * EDGE:]

    def border_line(k):
        return pl.ds(k * (R - 1) * WP, WP)

    def border_dot(frames, rows, taps):
        lhs = jnp.concatenate([F1[a, row] for a in frames for row in rows], axis=1)
        rhs = jnp.concatenate([w[0, a, p] for a in frames for p in taps], axis=0)
        return fold_ring(jnp.dot(lhs, rhs, preferred_element_type=f32))

    def border_own(frames):
        for k in range(2):
            acc1[border_line(k)] = border_dot(frames, ((1, 2), (R - 1, R))[k], ((1, 2), (0, 1))[k])

    def border_halo(frames, k):
        acc1[border_line(k)] += border_dot(frames, (k * (R + 1),), (2 * k,))

    def coarse(frames):
        for parity in range(2):
            lhs = jnp.concatenate(
                [ref[pl.ds(parity + b, HR)].reshape(HR * HP, CH) for ref in frames for b in range(2)],
                axis=1)
            z = jnp.dot(lhs, wu[parity, pl.ds(0, 2 * CH * len(frames))], preferred_element_type=f32)
            for i in range(HR):
                zi = z[i * HP:(i + 1) * HP]
                even = zi[:, :CH] + pltpu.roll(zi[:, 2 * CH:3 * CH], 1, 0)
                odd = zi[:, CH:2 * CH] + pltpu.roll(zi[:, 3 * CH:], HP - 1, 0)
                base = (2 * i + parity) * WP
                for at, n, to in ((0, HW, 0), (HW, EDGE // 2, W), (HP - EDGE // 2, EDGE // 2, WP - EDGE)):
                    for k, y in ((0, even), (1, odd)):
                        acc1[pl.ds(base + to + k, n, stride=2), :] += y[at:at + n]

    def act_two(row):
        y = acc1[pl.ds(row * WP, WP)] + b1[...]
        y = y / (1.0 + jnp.exp(-y))
        F2[2, 1 + row, pl.ds(0, W)] = y[:W].astype(bf)
        F2[2, 1 + row, pl.ds(W, EDGE)] = jnp.where(right_ok, y[W:W + EDGE], 0.0).astype(bf)
        F2[2, 1 + row, pl.ds(W + EDGE, EDGE)] = jnp.where(left_ok, y[W + EDGE:], 0.0).astype(bf)

    def inner(k, carry):
        act_two(1 + k)
        return carry

    def act_inside():
        lax.fori_loop(0, R - 2, inner, 0)

    for cp in one_cp:
        cp.wait()

    @pl.when(second)
    def _():
        inside_main((0,))
        sides("recv", ONE, tall_ds)
        to_first[1].start()
        to_first[2].start()
        sides("recv", ONE, col_ds)
        inside_rim((0,))
        border_own((0,))
        for k in range(2):
            border_halo((0,), k)
        sides("recv", COARSE, range(8))
        cross("recv", COARSE, col_ds)
        for i in (0, 4, 5):
            to_second[i].wait_recv()
        coarse((CA, CB))

    @pl.when(first)
    def _():
        to_first[0].wait_recv()
        inside_main((0, 1))
        sides("recv", ONE, col_ds)
        cross("recv", ONE, col_ds)
        inside_rim((0, 1))
        border_own((0, 1))
        sides("recv", COARSE, range(8))
        to_second[4].start()
        to_second[5].start()
        coarse((CA,))
        act_inside()
        to_second[3].start()
        sides("recv", ONE, tall_ds)
        to_first[1].wait_recv()
        to_first[2].wait_recv()

    def part_copy(k):
        return pltpu.make_async_remote_copy(
            src_ref=ps.at[k], dst_ref=pr.at[1 - k], send_sem=part_send.at[k],
            recv_sem=part_recv.at[1 - k], device_id={"row": r - 1 + 2 * k}, device_id_type=MESH)

    reach = (up_ok, down_ok)

    def send_part(k):
        lhs = jnp.concatenate([F2[a, 1 + k * (R - 1)] for a in range(3)], axis=1)
        rhs = jnp.concatenate([w[1, a, 2 - 2 * k] for a in range(3)], axis=0)
        ps[k] = fold_ring(jnp.dot(lhs, rhs, preferred_element_type=f32))[:W].astype(bf)

        @pl.when(reach[k])
        def _():
            part_copy(k).start()

    @pl.when(first)
    def _():
        sides("recv", TWO, col_ds)
        cross("recv", TWO, col_ds)
        to_first[3].wait_recv()
        for k in range(2):
            border_halo((0, 1), k)
            act_two(k * (R - 1))
            to_second[1 + k].start()
            send_part(k)

    @pl.when(second)
    def _():
        for k in range(2):
            act_two(k * (R - 1))
        act_inside()
        sides("recv", TWO, col_ds)
        for k in range(2):
            to_second[1 + k].wait_recv()
            send_part(k)

    when_second(to_second[3].wait_recv)
    lhs = jnp.concatenate(
        [F2[a, pl.ds(p, R), pl.ds(W, 2 * EDGE)].reshape(R * 2 * EDGE, CH)
         for a in range(3) for p in range(3)], axis=1)
    z = jnp.dot(lhs, weights(1, range(3)), preferred_element_type=f32)
    for n in range(R):
        part = z[n * 2 * EDGE:(n + 1) * 2 * EDGE]
        acc2[n, pl.ds(0, 1)] += part[2 * EDGE - 1:, :CH]
        acc2[n, pl.ds(W - 1, 1)] += part[:1, 2 * CH:]

    def finish(row, y):
        y = y + b2[...] + up[row // 2].astype(f32)
        out_v[0, row] = y.astype(bf)

    for n, y in enumerate(second_main((1, 2))):
        if 0 < n < R - 1:
            finish(n, acc2[n] + y)
        else:
            acc2[n] += y
    for k in range(2):
        row = k * (R - 1)

        @pl.when(reach[k])
        def _():
            part_copy(1 - k).wait_recv()
            acc2[row] += pr[k].astype(f32)

        finish(row, acc2[row])

    for cv, ds in ((ONE, range(8)), (COARSE, range(8)), (TWO, col_ds)):
        sides("send", cv, ds)
        cross("send", cv, col_ds)
    when_second(*[cp.wait_send for cp in to_first])
    when_first(*[cp.wait_send for cp in to_second])
    for k in range(2):
        @pl.when(reach[k])
        def _():
            part_copy(k).wait_send()


def store(src, dst, sem):
    cp = pltpu.make_async_copy(src, dst, sem)
    cp.start()
    cp.wait()


def per_device(latent, proj_weight, proj_bias, cache_one, cache_two,
               conv_one, bias_one, conv_two, bias_two):
    _, R, W, CH = cache_one.shape
    _, HR, HW, LCH = latent.shape
    WP, HP = W + 2 * EDGE, HW + 2 * EDGE
    anywhere = pl.BlockSpec(memory_space=pl.ANY)
    bf, f32 = jnp.bfloat16, jnp.float32
    dma = pltpu.SemaphoreType.DMA
    decoded = pl.pallas_call(
        functools.partial(kernel, lax.axis_size("row"), lax.axis_size("col")),
        out_shape=pltpu.VMEM(cache_one.shape, bf),
        in_specs=[anywhere] * 9,
        out_specs=pl.BlockSpec(memory_space=pltpu.VMEM),
        scratch_shapes=[
            pltpu.VMEM((HR, HW, LCH), bf),
            pltpu.VMEM((LCH, CH), bf),
            pltpu.VMEM((2, 3, 3, CH, 3 * CH), bf),
            pltpu.VMEM((2, 4 * CH, 4 * CH), bf),
            pltpu.VMEM((2, R + 2, WP, CH), bf),
            pltpu.VMEM((HR + 2, HP, CH), bf),
            pltpu.VMEM((HR + 2, HP, CH), bf),
            pltpu.VMEM((3, R + 2, WP, CH), bf),
            pltpu.VMEM((HR, W, CH), bf),
            pltpu.VMEM((R * WP, CH), f32),
            pltpu.VMEM((R, W, CH), f32),
            pltpu.VMEM((W, CH), f32),
            pltpu.VMEM((2, W, CH), bf),
            pltpu.VMEM((2, W, CH), bf),
            pltpu.VMEM((1, CH), f32),
            pltpu.VMEM((1, CH), f32),
            pltpu.VMEM((1, CH), f32),
            dma((13,)), dma((3, 8)), dma((3, 8)), dma((3, 2)), dma((3, 2)),
            dma((2, 3)), dma((2, 3)), dma((2,)), dma((2,)),
        ],
        compiler_params=pltpu.CompilerParams(
            collective_id=0, has_side_effects=True, vmem_limit_bytes=60 * 1024 * 1024),
        name="decoder_window",
    )(latent, proj_weight, proj_bias.reshape(1, CH), cache_one, cache_two,
      conv_one, bias_one.reshape(1, CH), conv_two, bias_two.reshape(1, CH))
    return pl.pallas_call(
        store,
        out_shape=jax.ShapeDtypeStruct(cache_one.shape, bf),
        in_specs=[pl.BlockSpec(memory_space=pltpu.VMEM)],
        out_specs=anywhere,
        scratch_shapes=[dma],
        compiler_params=pltpu.CompilerParams(vmem_limit_bytes=1024 * 1024),
        name="store",
    )(decoded)


def solution(mesh):
    placed = P(("grp", "frm"), "row", "col", None)
    return jax.shard_map(
        per_device,
        mesh=mesh,
        in_specs=(placed, P(), P(), placed, placed, P(), P(), P(), P()),
        out_specs=placed,
        check_vma=False,
    )
```

```python
import functools

import jax
import jax.numpy as jnp
from jax import lax
from jax.experimental import pallas as pl
from jax.experimental.pallas import tpu as pltpu
from jax.sharding import PartitionSpec as P

EDGE = 16
MESH = pl.DeviceIdType.MESH
SIDES = [(-1, 0), (1, 0), (0, -1), (0, 1), (-1, -1), (-1, 1), (1, -1), (1, 1)]
ONE, COARSE, TWO = 0, 1, 2
MIDDLE = (1, 0, 1)


def kernel(rows_n, cols_n, lat_h, pw_h, pb_h, c1_h, c2_h, w1_h, b1_h, w2_h, b2_h, out_v,
           lat, pw, w, wu, F1, CA, CB, F2, up, acc1, acc2, s1, ps, pr, pb, b1, b2,
           load_sem, side_send, side_recv, cross_send, cross_recv,
           mid_send, mid_recv, part_send, part_recv):
    R, W, CH = c1_h.shape[1], c1_h.shape[2], c1_h.shape[3]
    HR, HW = lat.shape[0], lat.shape[1]
    WP, HP = W + 2 * EDGE, HW + 2 * EDGE
    bf, f32 = jnp.bfloat16, jnp.float32
    r, c, f = lax.axis_index("row"), lax.axis_index("col"), lax.axis_index("frm")
    up_ok, down_ok = r > 0, r < rows_n - 1
    left_ok, right_ok = c > 0, c < cols_n - 1
    first, second = f == 0, f == 1

    def exists(d):
        dr, dc = SIDES[d]
        ok = None
        for test in ([up_ok] if dr < 0 else [down_ok] if dr > 0 else []) + (
                [left_ok] if dc < 0 else [right_ok] if dc > 0 else []):
            ok = test if ok is None else jnp.logical_and(ok, test)
        return ok

    def where_is(d):
        dr, dc = SIDES[d]
        ids = {}
        if dr:
            ids["row"] = r + dr
        if dc:
            ids["col"] = c + dc
        return ids

    def opposite(d):
        return SIDES.index((-SIDES[d][0], -SIDES[d][1]))

    loads = []

    def load(src, dst):
        cp = pltpu.make_async_copy(src, dst, load_sem.at[len(loads)])
        cp.start()
        loads.append(cp)
        return cp

    def load_weights(cv, src):
        return [load(src.at[:, :, q], w.at[cv, :, :, :, pl.ds(q * CH, CH)]) for q in range(3)]

    first_cp = [load(lat_h.at[0], lat), load(pw_h, pw), load(pb_h, pb)]
    two_cp = [load(c2_h.at[0], F2.at[0, pl.ds(1, R), pl.ds(0, W)])] + load_weights(1, w2_h)
    w_cp = load_weights(0, w1_h)
    one_cp = [load(c1_h.at[0], F1.at[0, pl.ds(1, R), pl.ds(0, W)]), load(b1_h, b1), load(b2_h, b2)]

    partner = {"frm": 1 - f}
    barrier = pltpu.get_barrier_semaphore()
    for d in range(8):
        @pl.when(exists(d))
        def _():
            for ids in ({}, partner)[:2 if SIDES[d][0] == 0 else 1]:
                pl.semaphore_signal(barrier, inc=1, device_id={**where_is(d), **ids},
                                    device_id_type=MESH)
    pl.semaphore_signal(barrier, inc=1, device_id=partner, device_id_type=MESH)

    def clear(ref, *place):
        shape = ref.at[place].shape
        ref[place] = jnp.zeros(shape, bf)

    rims = ((left_ok, lambda n: pl.ds(n - EDGE, EDGE)), (right_ok, lambda n: pl.ds(n - 2 * EDGE, EDGE)))
    for ref, tall, wide in ((F1.at[0], R, WP), (CA, HR, HP)):
        for ok, row in ((up_ok, 0), (down_ok, tall + 1)):
            @pl.when(jnp.logical_not(ok))
            def _():
                clear(ref, row, pl.ds(0, wide))
        for ok, rim in rims:
            @pl.when(jnp.logical_not(ok))
            def _():
                clear(ref, pl.ds(0, tall + 2), rim(wide))
    for ok, rim in rims:
        @pl.when(jnp.logical_not(ok))
        def _():
            clear(F2, 0, pl.ds(1, R), rim(WP))

            @pl.when(first)
            def _():
                clear(F1, 1, pl.ds(1, R), rim(WP))
                clear(F2, 1, pl.ds(1, R), rim(WP))

            @pl.when(second)
            def _():
                clear(CB, pl.ds(1, HR), rim(HP))
    for a in range(3):
        for row in (0, R + 1):
            clear(F2, a, row, pl.ds(0, WP))

    for cp in first_cp:
        cp.wait()

    def project(i, carry):
        v = jnp.dot(lat[i], pw[...], preferred_element_type=f32) + pb[...]
        v = v.astype(bf).astype(f32)
        CA[1 + i, pl.ds(0, HW)] = (v / (1.0 + jnp.exp(-v))).astype(bf)
        for k in range(2):
            s1[pl.ds(k, HW, stride=2), :] = v
        up[i] = s1[...].astype(bf)
        return carry

    lax.fori_loop(0, HR, project, 0)

    def side_refs(cv, d, slot=0):
        dr, dc = SIDES[d]
        n, m = (HR, HW) if cv == COARSE else (R, W)
        row, land_row = (0, n + 1) if dr < 0 else (n - 1, 0)
        col, land_col = ((0, m) if dc < 0 else (m - EDGE, m + EDGE))
        rows, land_rows = (pl.ds(row, 1), pl.ds(land_row, 1)) if dr else (pl.ds(0, n), pl.ds(1, n))
        cols, land_cols = (
            (pl.ds(col, EDGE), pl.ds(land_col, EDGE)) if dc else (pl.ds(0, m), pl.ds(0, m)))
        if cv == COARSE:
            src = CA.at[pl.ds(1 + rows.start, rows.size), cols]
            return src, (CB if slot else CA).at[land_rows, land_cols]
        src = (c1_h, c2_h)[cv // 2].at[0, rows, cols]
        return src, (F1, F2)[cv // 2].at[slot, land_rows, land_cols]

    def side_copy(cv, d):
        src, dst = side_refs(cv, d)
        return pltpu.make_async_remote_copy(
            src_ref=src, dst_ref=dst, send_sem=side_send.at[cv, d], recv_sem=side_recv.at[cv, d],
            device_id=where_is(d), device_id_type=MESH)

    def cross_copy(cv, d):
        src, dst = side_refs(cv, d, 1)
        return pltpu.make_async_remote_copy(
            src_ref=src, dst_ref=dst, send_sem=cross_send.at[cv, d - 2],
            recv_sem=cross_recv.at[cv, d - 2], device_id={**where_is(d), **partner},
            device_id_type=MESH)

    col_ds, from_rows = (2, 3), ((1, 6, 7), (0, 4, 5))

    def sides(act, cv, ds):
        for d in ds:
            @pl.when(exists(opposite(d) if act == "recv" else d))
            def _():
                cp = side_copy(cv, d)
                {"start": cp.start, "recv": cp.wait_recv, "send": cp.wait_send}[act]()

    def cross(act, cv, ds):
        owner = f == MIDDLE[cv]
        for d in ds:
            there = exists(opposite(d) if act == "recv" else d)

            @pl.when(jnp.logical_and(there, jnp.logical_not(owner) if act == "recv" else owner))
            def _():
                cp = cross_copy(cv, d)
                {"start": cp.start, "recv": cp.wait_recv, "send": cp.wait_send}[act]()

    def to_partner(cv, k, src, dst):
        return pltpu.make_async_remote_copy(
            src_ref=src, dst_ref=dst, send_sem=mid_send.at[cv, k], recv_sem=mid_recv.at[cv, k],
            device_id=partner, device_id_type=MESH)

    all_w, all_h = pl.ds(0, WP), pl.ds(0, HP)
    to_first = [
        to_partner(0, 0, c1_h.at[0], F1.at[1, pl.ds(1, R), pl.ds(0, W)]),
        to_partner(0, 1, F1.at[0, 0, all_w], F1.at[1, 0, all_w]),
        to_partner(0, 2, F1.at[0, R + 1, all_w], F1.at[1, R + 1, all_w]),
        to_partner(1, 0, c2_h.at[0], F2.at[1, pl.ds(1, R), pl.ds(0, W)])]
    main = pl.ds(1, HR), pl.ds(0, HW)
    to_second = [
        to_partner(0, 0, CA.at[main], CB.at[main]),
        to_partner(1, 0, F2.at[2, 1, all_w], F2.at[1, 1, all_w]),
        to_partner(1, 1, F2.at[2, R, all_w], F2.at[1, R, all_w]),
        to_partner(1, 2, F2.at[2, pl.ds(2, R - 2), all_w], F2.at[1, pl.ds(2, R - 2), all_w]),
        to_partner(0, 1, CA.at[0, all_h], CB.at[0, all_h]),
        to_partner(0, 2, CA.at[HR + 1, all_h], CB.at[HR + 1, all_h])]

    def when_first(*bodies):
        @pl.when(first)
        def _():
            for body in bodies:
                body()

    def when_second(*bodies):
        @pl.when(second)
        def _():
            for body in bodies:
                body()

    def weights(cv, frames):
        return jnp.concatenate([w[cv, a].reshape(3 * CH, 3 * CH) for a in frames], axis=0)

    def fold_taps(place, a):
        k0, k1, k2 = (w[0, a, p].astype(f32) for p in range(3))
        for parity, pair in ((0, (k0, k1 + k2)), (1, (k0 + k1, k2))):
            for b, m in enumerate(pair):
                q0, q1, q2 = m[:, :CH], m[:, CH:2 * CH], m[:, 2 * CH:]
                wu[parity, pl.ds((2 * place + b) * CH, CH)] = jnp.concatenate(
                    [q1 + q2, q0 + q1, q0, q2], axis=1).astype(bf)

    spot = lax.broadcasted_iota(jnp.int32, (8, CH), 0)

    def fold_main(z):
        after = pltpu.roll(z[:, :CH], 1, 0)
        after = jnp.concatenate([jnp.where(spot == 0, 0.0, after[:8]), after[8:]], axis=0)
        ahead = pltpu.roll(z[:, 2 * CH:], W - 1, 0)
        ahead = jnp.concatenate([ahead[:W - 8], jnp.where(spot == 7, 0.0, ahead[W - 8:])], axis=0)
        return after + z[:, CH:2 * CH] + ahead

    def fold_ring(z):
        n = z.shape[0]
        return pltpu.roll(z[:, :CH], 1, 0) + z[:, CH:2 * CH] + pltpu.roll(z[:, 2 * CH:], n - 1, 0)

    def second_main(frames, at=0, size=R):
        lhs = jnp.concatenate(
            [F2[a, pl.ds(at + p, size), pl.ds(0, W)].reshape(size * W, CH)
             for a in frames for p in range(3)], axis=1)
        z = jnp.dot(lhs, weights(1, frames), preferred_element_type=f32)
        return [fold_main(z[n * W:(n + 1) * W]) for n in range(size)]

    def own_two(at, size):
        for n, y in enumerate(second_main((0,), at, size)):
            acc2[at + n] = y

    tall = 1 + up_ok.astype(jnp.int32) + down_ok.astype(jnp.int32)
    wide = 1 + left_ok.astype(jnp.int32) + right_ok.astype(jnp.int32)
    pl.semaphore_wait(barrier, tall * wide + wide - 1)
    sides("start", ONE, (4, 5, 6, 7))
    sides("start", COARSE, (4, 5, 6, 7))
    when_second(lambda: sides("start", ONE, (0, 1)))
    sides("start", ONE, col_ds)
    cross("start", ONE, col_ds)
    when_second(to_first[0].start)
    when_first(to_second[0].start)
    sides("start", COARSE, (0, 1, 2, 3))
    cross("start", COARSE, col_ds)
    when_first(lambda: sides("start", ONE, (0, 1)))

    for cp in two_cp:
        cp.wait()
    own_two(0, R)
    when_second(to_first[3].start)
    sides("start", TWO, col_ds)
    cross("start", TWO, col_ds)

    for cp in w_cp:
        cp.wait()
    fold_taps(0, 2)
    when_second(lambda: fold_taps(1, 1))

    def inside_dot(frames, at, n):
        lhs = jnp.concatenate(
            [F1[a, pl.ds(1 + p, R - 2), pl.ds(at, n)].reshape((R - 2) * n, CH)
             for a in frames for p in range(3)], axis=1)
        z = jnp.dot(lhs, weights(0, frames), preferred_element_type=f32)
        return [z[k * n:(k + 1) * n] for k in range(R - 2)]

    def inside_main(frames):
        for k, z in enumerate(inside_dot(frames, 0, W)):
            z = jnp.concatenate([z, jnp.zeros((2 * EDGE, 3 * CH), f32)], axis=0)
            acc1[pl.ds((1 + k) * WP, WP)] = fold_ring(z)

    def inside_rim(frames):
        rest = jnp.zeros((EDGE, 3 * CH), f32)
        for k, z in enumerate(inside_dot(frames, W, 2 * EDGE)):
            y = fold_ring(jnp.concatenate([rest, z, rest], axis=0))
            acc1[pl.ds((1 + k) * WP + W - EDGE, 3 * EDGE)] += y[:3 * EDGE]
            acc1[pl.ds((1 + k) * WP, EDGE)] += y[3 * EDGE:]

    def border_line(k):
        return pl.ds(k * (R - 1) * WP, WP)

    def border_dot(frames, rows, taps):
        lhs = jnp.concatenate([F1[a, row] for a in frames for row in rows], axis=1)
        rhs = jnp.concatenate([w[0, a, p] for a in frames for p in taps], axis=0)
        return fold_ring(jnp.dot(lhs, rhs, preferred_element_type=f32))

    def border_own(frames):
        for k in range(2):
            acc1[border_line(k)] = border_dot(frames, ((1, 2), (R - 1, R))[k], ((1, 2), (0, 1))[k])

    def border_halo(frames, k):
        acc1[border_line(k)] += border_dot(frames, (k * (R + 1),), (2 * k,))

    def coarse(frames):
        for parity in range(2):
            lhs = jnp.concatenate(
                [ref[pl.ds(parity + b, HR)].reshape(HR * HP, CH) for ref in frames for b in range(2)],
                axis=1)
            z = jnp.dot(lhs, wu[parity, pl.ds(0, 2 * CH * len(frames))], preferred_element_type=f32)
            for i in range(HR):
                zi = z[i * HP:(i + 1) * HP]
                even = zi[:, :CH] + pltpu.roll(zi[:, 2 * CH:3 * CH], 1, 0)
                odd = zi[:, CH:2 * CH] + pltpu.roll(zi[:, 3 * CH:], HP - 1, 0)
                base = (2 * i + parity) * WP
                for at, n, to in ((0, HW, 0), (HW, EDGE // 2, W), (HP - EDGE // 2, EDGE // 2, WP - EDGE)):
                    for k, y in ((0, even), (1, odd)):
                        acc1[pl.ds(base + to + k, n, stride=2), :] += y[at:at + n]

    def act_two(row):
        y = acc1[pl.ds(row * WP, WP)] + b1[...]
        y = y / (1.0 + jnp.exp(-y))
        F2[2, 1 + row, pl.ds(0, W)] = y[:W].astype(bf)
        F2[2, 1 + row, pl.ds(W, EDGE)] = jnp.where(right_ok, y[W:W + EDGE], 0.0).astype(bf)
        F2[2, 1 + row, pl.ds(W + EDGE, EDGE)] = jnp.where(left_ok, y[W + EDGE:], 0.0).astype(bf)

    def inner(k, carry):
        act_two(1 + k)
        return carry

    def act_inside():
        lax.fori_loop(0, R - 2, inner, 0)

    for cp in one_cp:
        cp.wait()

    @pl.when(second)
    def _():
        inside_main((0,))
        for k in range(2):
            sides("recv", ONE, from_rows[k])
            to_first[1 + k].start()
        sides("recv", ONE, col_ds)
        inside_rim((0,))
        border_own((0,))
        for k in range(2):
            border_halo((0,), k)
        sides("recv", COARSE, range(8))
        cross("recv", COARSE, col_ds)
        for i in (0, 4, 5):
            to_second[i].wait_recv()
        coarse((CA, CB))

    @pl.when(first)
    def _():
        to_first[0].wait_recv()
        inside_main((0, 1))
        sides("recv", ONE, col_ds)
        cross("recv", ONE, col_ds)
        inside_rim((0, 1))
        border_own((0, 1))
        sides("recv", COARSE, range(8))
        to_second[4].start()
        to_second[5].start()
        coarse((CA,))
        act_inside()
        to_second[3].start()

    def part_copy(k):
        return pltpu.make_async_remote_copy(
            src_ref=ps.at[k], dst_ref=pr.at[1 - k], send_sem=part_send.at[k],
            recv_sem=part_recv.at[1 - k], device_id={"row": r - 1 + 2 * k}, device_id_type=MESH)

    reach = (up_ok, down_ok)

    def send_part(k):
        lhs = jnp.concatenate([F2[a, 1 + k * (R - 1)] for a in range(3)], axis=1)
        rhs = jnp.concatenate([w[1, a, 2 - 2 * k] for a in range(3)], axis=0)
        ps[k] = fold_ring(jnp.dot(lhs, rhs, preferred_element_type=f32))[:W].astype(bf)

        @pl.when(reach[k])
        def _():
            part_copy(k).start()

    @pl.when(first)
    def _():
        sides("recv", TWO, col_ds)
        cross("recv", TWO, col_ds)
        to_first[3].wait_recv()
        for k in range(2):
            sides("recv", ONE, from_rows[k])
            to_first[1 + k].wait_recv()
            border_halo((0, 1), k)
            act_two(k * (R - 1))
            to_second[1 + k].start()
            send_part(k)

    @pl.when(second)
    def _():
        for k in range(2):
            act_two(k * (R - 1))
        act_inside()
        sides("recv", TWO, col_ds)
        for k in range(2):
            to_second[1 + k].wait_recv()
            send_part(k)

    when_second(to_second[3].wait_recv)
    lhs = jnp.concatenate(
        [F2[a, pl.ds(p, R), pl.ds(W, 2 * EDGE)].reshape(R * 2 * EDGE, CH)
         for a in range(3) for p in range(3)], axis=1)
    z = jnp.dot(lhs, weights(1, range(3)), preferred_element_type=f32)
    for n in range(R):
        part = z[n * 2 * EDGE:(n + 1) * 2 * EDGE]
        acc2[n, pl.ds(0, 1)] += part[2 * EDGE - 1:, :CH]
        acc2[n, pl.ds(W - 1, 1)] += part[:1, 2 * CH:]

    def finish(row, y):
        y = y + b2[...] + up[row // 2].astype(f32)
        out_v[0, row] = y.astype(bf)

    for n, y in enumerate(second_main((1, 2))):
        if 0 < n < R - 1:
            finish(n, acc2[n] + y)
        else:
            acc2[n] += y
    for k in range(2):
        row = k * (R - 1)

        @pl.when(reach[k])
        def _():
            part_copy(1 - k).wait_recv()
            acc2[row] += pr[k].astype(f32)

        finish(row, acc2[row])

    for cv, ds in ((ONE, range(8)), (COARSE, range(8)), (TWO, col_ds)):
        sides("send", cv, ds)
        cross("send", cv, col_ds)
    when_second(*[cp.wait_send for cp in to_first])
    when_first(*[cp.wait_send for cp in to_second])
    for k in range(2):
        @pl.when(reach[k])
        def _():
            part_copy(k).wait_send()


def store(src, dst, sem):
    cp = pltpu.make_async_copy(src, dst, sem)
    cp.start()
    cp.wait()


def per_device(latent, proj_weight, proj_bias, cache_one, cache_two,
               conv_one, bias_one, conv_two, bias_two):
    _, R, W, CH = cache_one.shape
    _, HR, HW, LCH = latent.shape
    WP, HP = W + 2 * EDGE, HW + 2 * EDGE
    anywhere = pl.BlockSpec(memory_space=pl.ANY)
    bf, f32 = jnp.bfloat16, jnp.float32
    dma = pltpu.SemaphoreType.DMA
    decoded = pl.pallas_call(
        functools.partial(kernel, lax.axis_size("row"), lax.axis_size("col")),
        out_shape=pltpu.VMEM(cache_one.shape, bf),
        in_specs=[anywhere] * 9,
        out_specs=pl.BlockSpec(memory_space=pltpu.VMEM),
        scratch_shapes=[
            pltpu.VMEM((HR, HW, LCH), bf),
            pltpu.VMEM((LCH, CH), bf),
            pltpu.VMEM((2, 3, 3, CH, 3 * CH), bf),
            pltpu.VMEM((2, 4 * CH, 4 * CH), bf),
            pltpu.VMEM((2, R + 2, WP, CH), bf),
            pltpu.VMEM((HR + 2, HP, CH), bf),
            pltpu.VMEM((HR + 2, HP, CH), bf),
            pltpu.VMEM((3, R + 2, WP, CH), bf),
            pltpu.VMEM((HR, W, CH), bf),
            pltpu.VMEM((R * WP, CH), f32),
            pltpu.VMEM((R, W, CH), f32),
            pltpu.VMEM((W, CH), f32),
            pltpu.VMEM((2, W, CH), bf),
            pltpu.VMEM((2, W, CH), bf),
            pltpu.VMEM((1, CH), f32),
            pltpu.VMEM((1, CH), f32),
            pltpu.VMEM((1, CH), f32),
            dma((13,)), dma((3, 8)), dma((3, 8)), dma((3, 2)), dma((3, 2)),
            dma((2, 3)), dma((2, 3)), dma((2,)), dma((2,)),
        ],
        compiler_params=pltpu.CompilerParams(
            collective_id=0, has_side_effects=True, vmem_limit_bytes=60 * 1024 * 1024),
        name="decoder_window",
    )(latent, proj_weight, proj_bias.reshape(1, CH), cache_one, cache_two,
      conv_one, bias_one.reshape(1, CH), conv_two, bias_two.reshape(1, CH))
    return pl.pallas_call(
        store,
        out_shape=jax.ShapeDtypeStruct(cache_one.shape, bf),
        in_specs=[pl.BlockSpec(memory_space=pltpu.VMEM)],
        out_specs=anywhere,
        scratch_shapes=[dma],
        compiler_params=pltpu.CompilerParams(vmem_limit_bytes=1024 * 1024),
        name="store",
    )(decoded)


def solution(mesh):
    placed = P(("grp", "frm"), "row", "col", None)
    return jax.shard_map(
        per_device,
        mesh=mesh,
        in_specs=(placed, P(), P(), placed, placed, P(), P(), P(), P()),
        out_specs=placed,
        check_vma=False,
    )
```
